1024 devices in a mesh: batch: 32 (over z, core), col: 4 (over x), rep: 8 (over y).
Axes of the slice: x: 4, y: 8, z: 16, core: 2. Of those that a mesh axis runs over, the one named last changes fastest.
Arguments:
- lookups: bfloat16 [262144, 1024], P(('rep', 'batch'), 'col'), parts along dimension 0, may hold values from -6 to 6
- input_weight: bfloat16 [1024, 1024], replicated, may hold values from -0.1875 to 0.1875
- joined_weight: bfloat16 [1024, 2048], replicated, may hold values from -0.1875 to 0.1875
- output_weight: bfloat16 [512, 1024], replicated, may hold values from -0.25 to 0.25
- owner_counts: int32 [1024, 32], P(('rep', 'batch', 'col')), parts along dimension 0, may hold values from 1 to 12, 256 in all within a row
- user_index: int32 [262144], P(('rep', 'batch', 'col')), parts along dimension 0, may hold values from 0 to 7
Outputs:
- layer_out: bfloat16 [262144, 1024], P(('rep', 'batch', 'col')), parts along dimension 0
The draws below stay inside these ranges and needn't reach their ends.
There are 8 independent parts, one for each index of `rep`. The reference program is written for one: setup_inputs(seed, part) draws one part's arguments, and reference() takes and returns one part's arrays. A program takes and returns all parts, laid end to end along the dimension named above; an argument that names none is the same for every part. Nothing has to cross between parts.
Inputs may be any that keep to these rules, and one draw needn't show every extreme that they name: `owner_counts`: each row sums to 256; every entry is 1 or more and each row reaches 12.
All inputs are finite; a program needn't handle non-finite values.
Results may differ from the reference program's by a relative error of at most 0.0071.
Values may be sent and summed in bfloat16 or wider, within the bound.
A program may use at most 32 MiB of HBM per device.

```python
import math
import jax
import jax.numpy as jnp
import numpy as np
from jax import lax

D = 1024
HEADS = 4
HEAD_DIM = 128
USERS = 8
TOK_DEV = 256
CAP = 12
TOKENS = 32768
N_BATCH = 32
N_COL = 4


def plant(array, stream_key, least, high):
    longest = array.shape.index(max(array.shape))
    spots = []
    for shift in (0, 1):
        where = [jax.random.randint(jax.random.fold_in(stream_key, axis), (), 0, length) for axis, length in enumerate(array.shape)]
        where[longest] = (where[longest] + shift) % array.shape[longest]
        spots.append(tuple(where))
    return array.at[spots[0]].set(least).at[spots[1]].set(high)


def levels(rng, shape, pieces, smallest, high):
    def one(axis_at, parts):
        draws = jax.random.uniform(jax.random.fold_in(jax.random.fold_in(rng, 6), axis_at), (parts,), jnp.float32, smallest / len(pieces), high / len(pieces))
        return jnp.repeat(jnp.exp(draws), shape[axis_at] // parts).reshape((-1,) + (1,) * (len(shape) - axis_at - 1))

    level = one(*pieces[0])
    for cut in pieces[1:]:
        level = level * one(*cut)
    return level


def cumulative_ranks(number_of, lean):
    portions = [(1 << 20) // math.isqrt(standing ** lean) + 1 for standing in range(1, number_of + 1)]
    scale = 1 + sum(portions) // (1 << 30)
    return np.cumsum(np.array([max(1, weight // scale) for weight in portions]))


def ranked_ids(rng, extent, count, slope):
    listing = cumulative_ranks(count, slope)
    pick = jax.random.randint(jax.random.fold_in(rng, 1), extent, 0, int(listing[count - 1]))
    grade = jnp.searchsorted(jnp.asarray(listing, jnp.int32), pick, side="right")
    return jax.random.permutation(jax.random.fold_in(rng, 2), count)[grade].astype(jnp.int32)


def length_profile(count, total, reach, lean):
    weights = [(1 << 20) // math.isqrt(rank ** lean) + 1 for rank in range(2, count + 1)]
    rest, given = total - reach - (count - 1), [1] * (count - 1)
    while rest > 0:
        candidates = [i for i in range(count - 1) if given[i] < reach]
        whole, budget = sum([weights[i] for i in candidates]), rest
        for i in candidates:
            addition = min(reach - given[i], max(1, budget * weights[i] // whole), rest)
            given[i] = given[i] + addition
            rest = rest - addition
    return np.array([reach] + given)


def uneven_parts(key, number_of, total, limit, lean):
    if number_of == 2:
        one = jax.random.randint(key, (), max(1, total - limit), min(limit, total - 1) + 1)
        return jnp.stack([one, total - one])
    lengths = jnp.asarray(length_profile(number_of, total, limit, lean), jnp.int32)
    pairs = (number_of - 1) // 2
    donor, taker = lengths[1:1 + 2 * pairs:2], lengths[2:2 + 2 * pairs:2]
    room = jnp.minimum(donor - 1, limit - taker)
    shifted = jax.random.randint(jax.random.fold_in(key, 1), (pairs,), 0, 1 << 20) % (room + 1)
    lengths = lengths.at[1:1 + 2 * pairs:2].set(donor - shifted).at[2:2 + 2 * pairs:2].set(taker + shifted)
    return lengths[jax.random.permutation(jax.random.fold_in(key, 2), number_of)]


def gaussian(stream_key, dims, deviation, most, cuts=(), kind=jnp.bfloat16):
    array = deviation * jax.random.normal(stream_key, dims, jnp.float32)
    if cuts:
        array = array * levels(stream_key, dims, cuts, -0.22, 0.18)
    return jnp.clip(array, -most, most).astype(kind)


def setup_inputs(seed: int = 0, part: int = 0) -> dict:
    splits = jax.random.split(jax.random.key(seed), 7)
    own_keys = jax.random.split(jax.random.fold_in(splits[6], part), 7)
    lookups = gaussian(own_keys[0], (TOKENS, D), 1.0, 6.0, ((0, 32), (1, 4)))
    input_weight = gaussian(splits[1], (D, D), D ** -0.5, 0.1875)
    joined_weight = gaussian(splits[2], (D, 4 * HEADS * HEAD_DIM), D ** -0.5, 0.1875)
    output_weight = gaussian(splits[3], (HEADS * HEAD_DIM, D), (HEADS * HEAD_DIM) ** -0.5, 0.25)
    owner_counts = jax.vmap(lambda own: uneven_parts(own, N_BATCH, TOK_DEV, CAP, 1))(jax.random.split(own_keys[4], (N_BATCH * N_COL))).reshape((N_BATCH * N_COL, N_BATCH)).astype(jnp.int32)
    user_index = plant(ranked_ids(own_keys[5], (TOKENS,), USERS, 2), jax.random.fold_in(own_keys[5], 3), 0, USERS - 1).astype(jnp.int32)
    return dict(lookups=lookups, input_weight=input_weight, joined_weight=joined_weight, output_weight=output_weight, owner_counts=owner_counts, user_index=user_index)


eps_norm = 1e-06

def layer_norm(values):
    row_mean = lax.optimization_barrier(jnp.mean(values, axis=-1, keepdims=True))
    centered = values - row_mean
    row_var = lax.optimization_barrier(jnp.mean(centered * centered, axis=-1, keepdims=True))
    return centered * lax.rsqrt(row_var + eps_norm)

def attend(joined_rows, seg_ids):
    width = HEADS * HEAD_DIM
    total = joined_rows.shape[0]
    gate_part = joined_rows[:, :width].astype(jnp.float32)
    value_part = joined_rows[:, width:2 * width].astype(jnp.float32).reshape(total, HEADS, HEAD_DIM)
    query_part = joined_rows[:, 2 * width:3 * width].astype(jnp.float32).reshape(total, HEADS, HEAD_DIM)
    key_part = joined_rows[:, 3 * width:].astype(jnp.float32).reshape(total, HEADS, HEAD_DIM)
    scores = jnp.einsum('ihd,jhd->hij', query_part, key_part) * HEAD_DIM ** (-0.5)
    positions = jnp.arange(total, dtype=jnp.int32)
    allowed = (positions[None, :] <= positions[:, None]) & (seg_ids[None, :] == seg_ids[:, None])
    weights = jnp.where(allowed[None], jax.nn.silu(scores), 0.0).astype(jnp.bfloat16)
    mixed = jnp.einsum('hij,jhd->ihd', weights.astype(jnp.float32), value_part).reshape(total, width)
    return (layer_norm(mixed) * gate_part).astype(jnp.bfloat16)

def reference(lookups, input_weight, joined_weight, output_weight, owner_counts, user_index):
    hidden = jnp.dot(lookups, input_weight, preferred_element_type=jnp.float32).astype(jnp.bfloat16)
    normed = layer_norm(hidden.astype(jnp.float32)).astype(jnp.bfloat16)
    joined = jax.nn.silu(jnp.dot(normed, joined_weight, preferred_element_type=jnp.float32)).astype(jnp.bfloat16)
    bin_starts = (jnp.cumsum(owner_counts, axis=1) - owner_counts).astype(jnp.int32)
    slot_ids = jnp.arange(CAP, dtype=jnp.int32)

    def owner_slots(owner_index):
        col_index = owner_index % N_COL
        dest_owner = owner_index // N_COL
        sources = (jnp.arange(N_BATCH, dtype=jnp.int32) * N_COL + col_index).astype(jnp.int32)
        counts = owner_counts[sources, dest_owner]
        offsets = bin_starts[sources, dest_owner]
        token_rows = (sources * TOK_DEV + offsets)[:, None] + slot_ids[None, :]
        filled = slot_ids[None, :] < counts[:, None]
        return (token_rows.reshape(-1).astype(jnp.int32), filled.reshape(-1))

    def per_owner(owner_index):
        token_rows, filled = owner_slots(owner_index)
        safe_rows = jnp.where(filled, token_rows, 0).astype(jnp.int32)
        seg_ids = jnp.where(filled, user_index[safe_rows], -1).astype(jnp.int32)
        gated = attend(joined[safe_rows], seg_ids)
        return jnp.dot(gated, output_weight, preferred_element_type=jnp.float32).astype(jnp.bfloat16)
    owner_ids = jnp.arange(N_BATCH * N_COL, dtype=jnp.int32)
    branches = lax.map(per_owner, owner_ids)
    token_rows, filled = jax.vmap(owner_slots)(owner_ids)
    targets = jnp.where(filled, token_rows, TOKENS).reshape(-1).astype(jnp.int32)
    placed = jnp.zeros((TOKENS, D), jnp.bfloat16).at[targets].set(branches.reshape(-1, D), mode='drop')
    return (hidden.astype(jnp.float32) + placed.astype(jnp.float32)).astype(jnp.bfloat16)
```

```python
import functools

import jax
import jax.numpy as jnp
from jax import lax
from jax.experimental import pallas as pl
from jax.experimental.pallas import tpu as pltpu
from jax.sharding import PartitionSpec as P

MESH = pl.DeviceIdType.MESH
HEADS = 4
HEAD_DIM = 128
WIDTH = HEADS * HEAD_DIM
D = 1024
CAP = 12
ROWS = 24
eps_norm = 1e-06
F32 = jnp.float32
BF16 = jnp.bfloat16

OFFSETS = [0] + [s * o for o in range(1, 8) for s in (1, -1)] + [8]
GROUPS = [(0, 6), (6, 10), (10, 14), (14, 16)]


def layer_norm(values):
    row_mean = jnp.mean(values, axis=-1, keepdims=True)
    centered = values - row_mean
    row_var = jnp.mean(centered * centered, axis=-1, keepdims=True)
    return centered * lax.rsqrt(row_var + eps_norm)


def silu(values):
    return values / (1.0 + jnp.exp(-values))


def dot(a, b):
    return jnp.dot(a, b, preferred_element_type=F32)


def dot_nt(a, b):
    return lax.dot_general(a, b, (((1,), (1,)), ((), ())), preferred_element_type=F32)


def iota(shape, dim):
    return lax.broadcasted_iota(jnp.int32, shape, dim)


def position(row, z, chips):
    a = row // ROWS
    i = row - a * ROWS
    step = (a + 1) // 2
    off = jnp.where((a & 1) == 1, step, chips - step)
    zz = z + off
    zz = jnp.where(zz >= chips, zz - chips, zz)
    zz = jnp.where(zz >= chips, zz - chips, zz)
    second = jnp.where(i < 16, i // 8, (i - 16) // 4)
    slot = jnp.where(i < 16, i & 7, 8 + (i & 3))
    return (2 * zz + second) * CAP + slot


def kernel(
    n, ncol, lk, win_h, wj_h, wo_h, cnt, usr, hid_o, br_o,
    tok, win, wj, wo, pay, rcv, sgp, sgr, joined, umat, mixed, rpay, rrcv,
    bar_x, wsem, lsem, xs, xr, gs, gr, fs, fr, bs, br,
):
    me = lax.axis_index("batch")
    col = lax.axis_index("col")
    chips = n // 2
    z, core = me // 2, lax.rem(me, 2)
    tokens = usr.shape[1]
    barrier = pltpu.get_barrier_semaphore()

    def sig_z(o, carry):
        pl.semaphore_signal(barrier, inc=1, device_id={"batch": lax.rem(me + o, n)}, device_id_type=MESH)
        return carry

    def sig_x(o, carry):
        pl.semaphore_signal(barrier, inc=1, device_id={"col": lax.rem(col + o, ncol)}, device_id_type=MESH)
        return carry

    lax.fori_loop(1, n, sig_z, 0)
    lax.fori_loop(1, ncol, sig_x, 0)

    weights = [
        pltpu.make_async_copy(win_h, win, wsem.at[0]),
        pltpu.make_async_copy(wj_h, wj, wsem.at[1]),
        pltpu.make_async_copy(wo_h, wo, wsem.at[2]),
    ]
    own_tok = pltpu.make_async_copy(lk.at[pl.ds(col * tokens, tokens)], tok.at[col], lsem.at[0])
    own_tok.start()
    for w in weights:
        w.start()

    counts = cnt[...].astype(F32)
    upto = (iota((n, n), 0) <= iota((n, n), 1)).astype(F32).astype(BF16)
    ends = dot(jnp.broadcast_to(counts, (8, n)).astype(BF16), upto)[0:1]
    starts = ends - counts
    rows = 8 * n
    row_d, row_r = iota((rows, n), 0) // 8, iota((rows, 1), 0) & 7
    mine = row_d == iota((rows, n), 1)
    start_col = jnp.sum(jnp.where(mine, starts, 0.0), axis=1, keepdims=True)
    count_col = jnp.sum(jnp.where(mine, counts, 0.0), axis=1, keepdims=True)
    lane_t = iota((rows, tokens), 1).astype(F32)
    first_r = row_r.astype(F32)
    last_r = 8.0 + (row_r & 3).astype(F32)
    pick_first = (lane_t == start_col + first_r) & (first_r < count_col)
    pick_last = (lane_t == start_col + last_r) & (last_r < count_col)
    users = usr[...].astype(F32) + 1.0
    seg_first = jnp.sum(jnp.where(pick_first, users, 0.0), axis=1, keepdims=True)
    seg_last = jnp.sum(jnp.where(pick_last, users, 0.0), axis=1, keepdims=True)
    lane = iota((rows, 128), 1)
    spread = jnp.where(lane == row_r, seg_first, 0.0) + jnp.where((lane == 8 + row_r) & (row_r < 4), seg_last, 0.0)
    own_rows = (iota((n, rows), 1) // 8 == iota((n, rows), 0)).astype(F32).astype(BF16)
    segs = dot(own_rows, spread.astype(BF16))
    for d in range(n):
        sgp[d] = segs[d : d + 1]

    pl.semaphore_wait(barrier, n - 1 + ncol - 1)

    def x_copy(o):
        peer = lax.rem(col + o, ncol)
        return pltpu.make_async_remote_copy(
            src_ref=lk.at[pl.ds(peer * tokens, tokens)], dst_ref=tok.at[col], send_sem=xs.at[o], recv_sem=xr.at[col],
            device_id={"col": peer}, device_id_type=MESH,
        )

    for o in range(1, ncol):
        x_copy(o).start()

    def z_copy(src, dst, send, recv, peer):
        return pltpu.make_async_remote_copy(
            src_ref=src.at[peer], dst_ref=dst.at[me], send_sem=send.at[peer], recv_sem=recv.at[me],
            device_id={"batch": peer}, device_id_type=MESH,
        )

    def z_wait(buf, send, recv, peer):
        pltpu.make_async_remote_copy(
            src_ref=buf.at[peer], dst_ref=buf.at[peer], send_sem=send.at[peer], recv_sem=recv.at[peer],
            device_id={"batch": peer}, device_id_type=MESH,
        ).wait_recv()

    partner = 2 * z + 1 - core

    def send_all(src, dst, send, recv):
        z_copy(src, dst, send, recv, partner).start()

        def step(o, carry):
            up, down = lax.rem(z + o, chips), lax.rem(z + chips - o, chips)
            for k in (0, 1):
                z_copy(src, dst, send, recv, 2 * up + k).start()
                z_copy(src, dst, send, recv, 2 * down + k).start()
            return carry

        lax.fori_loop(1, chips // 2, step, 0)
        across = lax.rem(z + chips // 2, chips)
        for k in (0, 1):
            z_copy(src, dst, send, recv, 2 * across + k).start()

    send_all(sgp, sgr, gs, gr)
    own_seg = pltpu.make_async_copy(sgp.at[me], sgr.at[me], lsem.at[1])
    own_seg.start()

    weights[0].wait()
    own_tok.wait()
    hidden = dot(tok[col], win[pl.ds(col * (D // ncol), D // ncol), :])
    for o in range(1, ncol):
        peer = lax.rem(col + o, ncol)
        pltpu.make_async_remote_copy(
            src_ref=tok.at[peer], dst_ref=tok.at[peer], send_sem=xs.at[o], recv_sem=xr.at[peer],
            device_id={"col": peer}, device_id_type=MESH,
        ).wait_recv()
        hidden += dot(tok[peer], win[pl.ds(peer * (D // ncol), D // ncol), :])
    hidden = hidden.astype(BF16)
    hid_o[...] = hidden

    first = dot(pick_first.astype(F32).astype(BF16), hidden)
    last = dot(pick_last.astype(F32).astype(BF16), hidden)
    pay[:, :, 0:D] = first.reshape(n, 8, D).astype(BF16)
    fold = jnp.where(row_r < 4, last[:, : D // 2], last[:, D // 2 :])
    pay[:, :, D:] = fold.reshape(n, 8, D // 2).astype(BF16)
    send_all(pay, rcv, fs, fr)
    own_pay = pltpu.make_async_copy(pay.at[me], rcv.at[me], lsem.at[2])
    own_pay.start()

    weights[1].wait()
    own_seg.wait()
    own_pay.wait()
    low = iota((8, 1), 0) < 4
    i24 = iota((ROWS, 128), 0)
    lane24 = iota((ROWS, 128), 1)
    want = jnp.where(i24 < 16, i24 & 7, 8 + (i24 & 3))
    is_a = (i24 < 8) | ((i24 >= 16) & (i24 < 20))

    for a0, a1 in GROUPS:
        parts = []
        for a in range(a0, a1):
            zz = lax.rem(z + (OFFSETS[a] + chips), chips)
            if a == 0:
                z_wait(sgr, gs, gr, partner)
                z_wait(rcv, fs, fr, partner)
            else:
                for k in (0, 1):
                    z_wait(sgr, gs, gr, 2 * zz + k)
                    z_wait(rcv, fs, fr, 2 * zz + k)
            va, vb = rcv[2 * zz].astype(F32), rcv[2 * zz + 1].astype(F32)
            ea, eb = va[:, D:], vb[:, D:]
            ex_lo = jnp.where(low, ea, pltpu.roll(eb, 4, 0))
            ex_hi = jnp.where(low, pltpu.roll(ea, 4, 0), eb)
            parts.append(jnp.concatenate([va[:, :D], vb[:, :D], jnp.concatenate([ex_lo, ex_hi], axis=1)], axis=0))
            seg = jnp.where(is_a, sgr[2 * zz], sgr[2 * zz + 1])
            seg = jnp.sum(jnp.where(lane24 == want, seg, 0.0), axis=1, keepdims=True)
            umat[a * ROWS : (a + 1) * ROWS, :] = jnp.where((lane24.astype(F32) == seg) & (lane24 > 0), 1.0, 0.0)
        r0, r1 = a0 * ROWS, a1 * ROWS
        normed = layer_norm(jnp.concatenate(parts, axis=0)).astype(BF16)

        def project(c, carry, normed=normed, r0=r0, r1=r1):
            cols = pl.ds(pl.multiple_of(c * WIDTH, WIDTH), WIDTH)
            joined[r0:r1, cols] = silu(dot(normed, wj[:, cols])).astype(BF16)
            return carry

        lax.fori_loop(0, 4, project, 0)

        u_all = umat[0:r1, :].astype(BF16)
        u_new = u_all[r0:r1]

        def allowed(ui, uj, i0, j0):
            shape = (ui.shape[0], uj.shape[0])
            pi = position(iota((shape[0], 1), 0) + i0, z, chips)
            pj = position(iota((1, shape[1]), 1) + j0, z, chips)
            return (dot_nt(ui, uj) > 0.5) & (pj <= pi)

        ok_new = allowed(u_all, u_new, 0, r0)
        ok_old = allowed(u_new, u_all[:r0], r0, 0) if r0 else None
        for h in range(HEADS):
            vs = slice(WIDTH + h * HEAD_DIM, WIDTH + (h + 1) * HEAD_DIM)
            qs = slice(2 * WIDTH + h * HEAD_DIM, 2 * WIDTH + (h + 1) * HEAD_DIM)
            ks = slice(3 * WIDTH + h * HEAD_DIM, 3 * WIDTH + (h + 1) * HEAD_DIM)
            hs = slice(h * HEAD_DIM, (h + 1) * HEAD_DIM)
            w = dot_nt(joined[0:r1, qs], joined[r0:r1, ks]) * HEAD_DIM ** (-0.5)
            w = jnp.where(ok_new, silu(w), 0.0).astype(BF16)
            add = dot(w, joined[r0:r1, vs])
            if r0:
                mixed[0:r0, hs] += add[:r0]
                w = dot_nt(joined[r0:r1, qs], joined[0:r0, ks]) * HEAD_DIM ** (-0.5)
                w = jnp.where(ok_old, silu(w), 0.0).astype(BF16)
                mixed[r0:r1, hs] = add[r0:] + dot(w, joined[0:r0, vs])
            else:
                mixed[0:r1, hs] = add

    for a0, a1 in GROUPS[::-1]:
        r0, r1 = a0 * ROWS, a1 * ROWS
        gated = layer_norm(mixed[r0:r1, :]) * joined[r0:r1, 0:WIDTH].astype(F32)
        for a in range(a0, a1)[::-1]:
            zz = lax.rem(z + (OFFSETS[a] + chips), chips)
            g = gated[(a - a0) * ROWS : (a - a0 + 1) * ROWS]
            e_lo, e_hi = g[16:24, : WIDTH // 2], g[16:24, WIDTH // 2 :]
            rpay[2 * zz, :, 0:WIDTH] = g[0:8].astype(BF16)
            rpay[2 * zz, :, WIDTH:] = jnp.where(low, e_lo, pltpu.roll(e_hi, 4, 0)).astype(BF16)
            rpay[2 * zz + 1, :, 0:WIDTH] = g[8:16].astype(BF16)
            rpay[2 * zz + 1, :, WIDTH:] = jnp.where(low, pltpu.roll(e_lo, 4, 0), e_hi).astype(BF16)
            if a == 0:
                z_copy(rpay, rrcv, bs, br, partner).start()
            else:
                for k in (0, 1):
                    z_copy(rpay, rrcv, bs, br, 2 * zz + k).start()
    own_ret = pltpu.make_async_copy(rpay.at[me], rrcv.at[me], lsem.at[3])
    own_ret.start()

    tok_t = iota((tokens, n), 0).astype(F32)
    dest = (tok_t >= starts) & (tok_t < ends)
    owner = jnp.sum(jnp.where(dest, iota((tokens, n), 1).astype(F32), 0.0), axis=1, keepdims=True)
    slot = jnp.sum(jnp.where(dest, tok_t - starts, 0.0), axis=1, keepdims=True)
    lane_p = iota((tokens, rows), 1)
    lane_i = lane_p & 7
    here = (lane_p // 8).astype(F32) == owner
    lane_f = lane_i.astype(F32)
    take_first = (here & (lane_f == slot)).astype(F32).astype(BF16)
    take_lo = (here & (lane_i < 4) & (lane_f + 8.0 == slot)).astype(F32).astype(BF16)
    take_hi = (here & (lane_i >= 4) & (lane_f + 4.0 == slot)).astype(F32).astype(BF16)

    own_ret.wait()
    weights[2].wait()

    def ret_wait(o, carry):
        z_wait(rrcv, bs, br, lax.rem(me + o, n))
        return carry

    lax.fori_loop(1, n, ret_wait, 0)
    back = rrcv[:, :, 0:WIDTH].astype(F32).reshape(rows, WIDTH).astype(BF16)
    back_x = rrcv[:, :, WIDTH:].astype(F32).reshape(rows, WIDTH // 2).astype(BF16)
    gated = dot(take_first, back)
    gated_lo = gated[:, : WIDTH // 2] + dot(take_lo, back_x)
    gated_hi = gated[:, WIDTH // 2 :] + dot(take_hi, back_x)
    branch = dot(gated_lo.astype(BF16), wo[: WIDTH // 2]) + dot(gated_hi.astype(BF16), wo[WIDTH // 2 :])
    br_o[...] = branch.astype(BF16)

    for o in range(1, ncol):
        x_copy(o).wait_send()

    def drain(o, carry):
        peer = lax.rem(me + o, n)
        z_copy(sgp, sgr, gs, gr, peer).wait_send()
        z_copy(pay, rcv, fs, fr, peer).wait_send()
        z_copy(rpay, rrcv, bs, br, peer).wait_send()
        return carry

    lax.fori_loop(1, n, drain, 0)


def on_device(n, ncol, lookups, input_weight, joined_weight, output_weight, owner_counts, user_index):
    tokens = user_index.shape[0]
    dma = pltpu.SemaphoreType.DMA
    anyspace = pl.BlockSpec(memory_space=pl.ANY)
    vmem = pl.BlockSpec(memory_space=pltpu.VMEM)
    hidden, branch = pl.pallas_call(
        functools.partial(kernel, n, ncol),
        name="hstu",
        out_shape=(jax.ShapeDtypeStruct((tokens, D), BF16), jax.ShapeDtypeStruct((tokens, D), BF16)),
        in_specs=[anyspace, anyspace, anyspace, anyspace, vmem, vmem],
        out_specs=(vmem, vmem),
        scratch_shapes=[
            pltpu.VMEM((ncol, tokens, D // ncol), BF16),
            pltpu.VMEM((D, D), BF16),
            pltpu.VMEM((D, 4 * WIDTH), BF16),
            pltpu.VMEM((WIDTH, D), BF16),
            pltpu.VMEM((n, 8, 3 * D // 2), BF16),
            pltpu.VMEM((n, 8, 3 * D // 2), BF16),
            pltpu.VMEM((n, 1, 128), F32),
            pltpu.VMEM((n, 1, 128), F32),
            pltpu.VMEM((n * CAP, 4 * WIDTH), BF16),
            pltpu.VMEM((n * CAP, 128), F32),
            pltpu.VMEM((n * CAP, WIDTH), F32),
            pltpu.VMEM((n, 8, 3 * WIDTH // 2), BF16),
            pltpu.VMEM((n, 8, 3 * WIDTH // 2), BF16),
            pltpu.SemaphoreType.REGULAR,
            dma((3,)), dma((4,)), dma((ncol,)), dma((ncol,)),
            dma((n,)), dma((n,)), dma((n,)), dma((n,)), dma((n,)), dma((n,)),
        ],
        compiler_params=pltpu.CompilerParams(collective_id=0, has_side_effects=True),
    )(lookups, input_weight, joined_weight, output_weight, owner_counts, user_index.reshape(1, tokens))
    return (hidden.astype(F32) + branch.astype(F32)).astype(BF16)


def solution(mesh):
    return jax.shard_map(
        functools.partial(on_device, mesh.shape["batch"], mesh.shape["col"]),
        mesh=mesh,
        in_specs=(
            P(("rep", "batch"), "col"),
            P(),
            P(),
            P(),
            P(("rep", "batch", "col"), None),
            P(("rep", "batch", "col")),
        ),
        out_specs=P(("rep", "batch", "col"), None),
        check_vma=False,
    )
```

```python
import functools

import jax
import jax.numpy as jnp
from jax import lax
from jax.experimental import pallas as pl
from jax.experimental.pallas import tpu as pltpu
from jax.sharding import PartitionSpec as P

MESH = pl.DeviceIdType.MESH
HEADS = 4
HEAD_DIM = 128
WIDTH = HEADS * HEAD_DIM
D = 1024
CAP = 12
ROWS = 24
eps_norm = 1e-06
F32 = jnp.float32
BF16 = jnp.bfloat16

OFFSETS = [0] + [s * o for o in range(1, 8) for s in (1, -1)] + [8]
REL = (0, 1, 3, 2)
RING = [1, 2, 3, 4, 5, 6, 7, 8]
GROUPS = [(0, 6), (6, 10), (10, 14), (14, 16)]


def layer_norm(values):
    row_mean = jnp.mean(values, axis=-1, keepdims=True)
    centered = values - row_mean
    row_var = jnp.mean(centered * centered, axis=-1, keepdims=True)
    return centered * lax.rsqrt(row_var + eps_norm)


def silu(values):
    return values / (1.0 + jnp.exp(-values))


def dot(a, b):
    return jnp.dot(a, b, preferred_element_type=F32)


def dot_nt(a, b):
    return lax.dot_general(a, b, (((1,), (1,)), ((), ())), preferred_element_type=F32)


def iota(shape, dim):
    return lax.broadcasted_iota(jnp.int32, shape, dim)


def position(row, z, chips):
    a = row // ROWS
    i = row - a * ROWS
    step = (a + 1) // 2
    off = jnp.where((a & 1) == 1, step, chips - step)
    zz = z + off
    zz = jnp.where(zz >= chips, zz - chips, zz)
    zz = jnp.where(zz >= chips, zz - chips, zz)
    second = jnp.where(i < 16, i // 8, (i - 16) // 4)
    slot = jnp.where(i < 16, i & 7, 8 + (i & 3))
    return (2 * zz + second) * CAP + slot


def kernel(
    n, ncol, lk, win_h, wj_h, wo_h, cnt, usr, out,
    tok, win, wj, wo, pay, rcv, sgp, sgr, joined, umat, mixed, rpay, rrcv,
    near2, near4, near8, wsem, lsem, xs, xr, gs, gr, fs, fr, bs, br,
):
    me = lax.axis_index("batch")
    col = lax.axis_index("col")
    chips = n // 2
    z, core = me // 2, lax.rem(me, 2)
    tokens = usr.shape[1]
    barrier = pltpu.get_barrier_semaphore()
    partner = 2 * z + 1 - core
    slab = D // ncol

    def at(o):
        return lax.rem(z + o + chips, chips)

    def signal(sem, peer):
        pl.semaphore_signal(sem, inc=1, device_id={"batch": peer}, device_id_type=MESH)

    for o in range(1, ncol):
        pl.semaphore_signal(barrier, inc=1, device_id={"col": lax.rem(col + o, ncol)}, device_id_type=MESH)
    signal(barrier, partner)
    for o in (1, -1):
        for k in (0, 1):
            signal(barrier, 2 * at(o) + k)

    own_tok = pltpu.make_async_copy(lk.at[pl.ds(col * tokens, tokens)], tok.at[0], lsem.at[0])
    own_tok.start()
    weights = [
        pltpu.make_async_copy(
            win_h.at[pl.ds(lax.rem(col + REL[j], ncol) * slab, slab)], win.at[pl.ds(j * slab, slab)], wsem.at[j]
        )
        for j in range(ncol)
    ]
    weights.append(pltpu.make_async_copy(wj_h, wj, wsem.at[ncol]))
    weights.append(pltpu.make_async_copy(wo_h, wo, wsem.at[ncol + 1]))
    for w in weights:
        w.start()

    counts = cnt[...].astype(F32)
    upto = (iota((n, n), 0) <= iota((n, n), 1)).astype(F32).astype(BF16)
    ends = dot(jnp.broadcast_to(counts, (8, n)).astype(BF16), upto)[0:1]
    starts = ends - counts
    rows = 8 * n
    row_d, row_r = iota((rows, n), 0) // 8, iota((rows, 1), 0) & 7
    mine = row_d == iota((rows, n), 1)
    start_col = jnp.sum(jnp.where(mine, starts, 0.0), axis=1, keepdims=True)
    count_col = jnp.sum(jnp.where(mine, counts, 0.0), axis=1, keepdims=True)
    lane_t = iota((rows, tokens), 1).astype(F32)
    first_r = row_r.astype(F32)
    last_r = 8.0 + (row_r & 3).astype(F32)
    pick_first = (lane_t == start_col + first_r) & (first_r < count_col)
    pick_last = (lane_t == start_col + last_r) & (last_r < count_col)
    users = usr[...].astype(F32) + 1.0
    seg_first = jnp.sum(jnp.where(pick_first, users, 0.0), axis=1, keepdims=True)
    seg_last = jnp.sum(jnp.where(pick_last, users, 0.0), axis=1, keepdims=True)
    lane = iota((rows, 128), 1)
    spread = jnp.where(lane == row_r, seg_first, 0.0) + jnp.where((lane == 8 + row_r) & (row_r < 4), seg_last, 0.0)
    own_rows = (iota((n, rows), 1) // 8 == iota((n, rows), 0)).astype(F32).astype(BF16)
    segs = dot(own_rows, spread.astype(BF16))
    for d in range(n):
        sgp[d] = segs[d : d + 1]

    pick_first = pick_first.astype(F32).astype(BF16)
    pick_last = pick_last.astype(F32).astype(BF16)

    def pack(j):
        first = dot(pick_first, tok[j])
        last = dot(pick_last, tok[j])
        fold = jnp.where(row_r < 4, last[:, : slab // 2], last[:, slab // 2 :])
        pay[:, j, :, 0:slab] = first.reshape(n, 8, slab).astype(BF16)
        pay[:, j, :, slab:] = fold.reshape(n, 8, slab // 2).astype(BF16)

    own_tok.wait()
    pack(0)

    pl.semaphore_wait(barrier, ncol - 1 + 5)
    for o in (1, -1):
        signal(near2, 2 * at(o) + core)

    def x_copy(o):
        peer = lax.rem(col + o, ncol)
        j = REL.index(ncol - o)
        return pltpu.make_async_remote_copy(
            src_ref=lk.at[pl.ds(peer * tokens, tokens)], dst_ref=tok.at[j], send_sem=xs.at[o], recv_sem=xr.at[j],
            device_id={"col": peer}, device_id_type=MESH,
        )

    for o in range(1, ncol):
        x_copy(o).start()

    def copy(src, dst, send, recv, peer):
        return pltpu.make_async_remote_copy(
            src_ref=src, dst_ref=dst, send_sem=send.at[peer], recv_sem=recv.at[me],
            device_id={"batch": peer}, device_id_type=MESH,
        )

    def z_copy(src, dst, send, recv, peer):
        return copy(src.at[peer], dst.at[me], send, recv, peer)

    def z_wait(buf, send, recv, peer):
        pltpu.make_async_remote_copy(
            src_ref=buf.at[peer], dst_ref=buf.at[peer], send_sem=send.at[peer], recv_sem=recv.at[peer],
            device_id={"batch": peer}, device_id_type=MESH,
        ).wait_recv()

    def send_own(peer):
        z_copy(sgp, sgr, gs, gr, peer).start()
        copy(pay.at[peer, pl.ds(0, 1)], rcv.at[me, pl.ds(0, 1)], fs, fr, peer).start()

    def send_rest(peer):
        copy(pay.at[peer, pl.ds(1, ncol - 1)], rcv.at[me, pl.ds(1, ncol - 1)], fs, fr, peer).start()

    def send_ring(send, offsets):
        for o in offsets:
            for k in (0, 1):
                send(2 * at(o) + k)
                if 2 * o != chips:
                    send(2 * at(-o) + k)

    send_own(partner)
    send_ring(send_own, [1])
    pl.semaphore_wait(near2, 2)
    for o in (2, -2):
        signal(near4, 2 * at(o) + core)
    send_ring(send_own, [2])
    pl.semaphore_wait(near4, 2)
    for o in (4, -4):
        signal(near8, 2 * at(o) + core)
    send_ring(send_own, [4, 3])
    own_seg = pltpu.make_async_copy(sgp.at[me], sgr.at[me], lsem.at[1])
    own_seg.start()
    pl.semaphore_wait(near8, 2)
    send_ring(send_own, [8, 7, 6, 5])

    for j in range(1, ncol):
        pltpu.make_async_remote_copy(
            src_ref=tok.at[j], dst_ref=tok.at[j], send_sem=xs.at[0], recv_sem=xr.at[j],
            device_id={"col": lax.rem(col + 1, ncol)}, device_id_type=MESH,
        ).wait_recv()
        pack(j)
    send_rest(partner)
    send_ring(send_rest, RING)
    own_pay = pltpu.make_async_copy(pay.at[me], rcv.at[me], lsem.at[2])
    own_pay.start()

    for w in weights[:ncol]:
        w.wait()
    hidden = dot(tok[0], win[0:slab])
    for j in range(1, ncol):
        hidden += dot(tok[j], win[j * slab : (j + 1) * slab])
    hidden = hidden.astype(BF16)
    weights[ncol].wait()
    own_seg.wait()
    own_pay.wait()
    low = iota((1, 8, 1), 1) < 4
    low8 = iota((8, 1), 0) < 4
    i24 = iota((ROWS, 128), 0)
    lane24 = iota((ROWS, 128), 1)
    want = jnp.where(i24 < 16, i24 & 7, 8 + (i24 & 3))
    is_a = (i24 < 8) | ((i24 >= 16) & (i24 < 20))

    for a0, a1 in GROUPS:
        parts = []
        for a in range(a0, a1):
            zz = lax.rem(z + (OFFSETS[a] + chips), chips)
            if a == 0:
                z_wait(sgr, gs, gr, partner)
                z_wait(rcv, fs, fr, partner)
            else:
                for k in (0, 1):
                    z_wait(sgr, gs, gr, 2 * zz + k)
                    z_wait(rcv, fs, fr, 2 * zz + k)
            va, vb = rcv[2 * zz].astype(F32), rcv[2 * zz + 1].astype(F32)
            ea, eb = va[:, :, slab:], vb[:, :, slab:]
            ex_lo = jnp.where(low, ea, pltpu.roll(eb, 4, 1))
            ex_hi = jnp.where(low, pltpu.roll(ea, 4, 1), eb)
            parts.append(jnp.concatenate([v[:, :, :slab] for v in (va, vb)] + [jnp.concatenate([ex_lo, ex_hi], axis=2)], axis=1))
            seg = jnp.where(is_a, sgr[2 * zz], sgr[2 * zz + 1])
            seg = jnp.sum(jnp.where(lane24 == want, seg, 0.0), axis=1, keepdims=True)
            umat[a * ROWS : (a + 1) * ROWS, :] = jnp.where((lane24.astype(F32) == seg) & (lane24 > 0), 1.0, 0.0)
        r0, r1 = a0 * ROWS, a1 * ROWS
        looked = jnp.concatenate(parts, axis=1).astype(BF16)
        projected = dot(looked[0], win[0:slab])
        for j in range(1, ncol):
            projected += dot(looked[j], win[j * slab : (j + 1) * slab])
        normed = layer_norm(projected.astype(BF16).astype(F32)).astype(BF16)

        def project(c, carry, normed=normed, r0=r0, r1=r1):
            cols = pl.ds(pl.multiple_of(c * WIDTH, WIDTH), WIDTH)
            joined[r0:r1, cols] = silu(dot(normed, wj[:, cols])).astype(BF16)
            return carry

        lax.fori_loop(0, 4, project, 0)

        u_all = umat[0:r1, :].astype(BF16)
        u_new = u_all[r0:r1]

        def allowed(ui, uj, i0, j0):
            shape = (ui.shape[0], uj.shape[0])
            pi = position(iota((shape[0], 1), 0) + i0, z, chips)
            pj = position(iota((1, shape[1]), 1) + j0, z, chips)
            return (dot_nt(ui, uj) > 0.5) & (pj <= pi)

        ok_new = allowed(u_all, u_new, 0, r0)
        ok_old = allowed(u_new, u_all[:r0], r0, 0) if r0 else None
        for h in range(HEADS):
            vs = slice(WIDTH + h * HEAD_DIM, WIDTH + (h + 1) * HEAD_DIM)
            qs = slice(2 * WIDTH + h * HEAD_DIM, 2 * WIDTH + (h + 1) * HEAD_DIM)
            ks = slice(3 * WIDTH + h * HEAD_DIM, 3 * WIDTH + (h + 1) * HEAD_DIM)
            hs = slice(h * HEAD_DIM, (h + 1) * HEAD_DIM)
            w = dot_nt(joined[0:r1, qs], joined[r0:r1, ks]) * HEAD_DIM ** (-0.5)
            w = jnp.where(ok_new, silu(w), 0.0).astype(BF16)
            add = dot(w, joined[r0:r1, vs])
            if r0:
                mixed[0:r0, hs] += add[:r0]
                w = dot_nt(joined[r0:r1, qs], joined[0:r0, ks]) * HEAD_DIM ** (-0.5)
                w = jnp.where(ok_old, silu(w), 0.0).astype(BF16)
                mixed[r0:r1, hs] = add[r0:] + dot(w, joined[0:r0, vs])
            else:
                mixed[0:r1, hs] = add

    for a0, a1 in GROUPS[::-1]:
        r0, r1 = a0 * ROWS, a1 * ROWS
        gated = layer_norm(mixed[r0:r1, :]) * joined[r0:r1, 0:WIDTH].astype(F32)
        for a in range(a0, a1)[::-1]:
            zz = lax.rem(z + (OFFSETS[a] + chips), chips)
            g = gated[(a - a0) * ROWS : (a - a0 + 1) * ROWS]
            e_lo, e_hi = g[16:24, : WIDTH // 2], g[16:24, WIDTH // 2 :]
            rpay[2 * zz, :, 0:WIDTH] = g[0:8].astype(BF16)
            rpay[2 * zz, :, WIDTH:] = jnp.where(low8, e_lo, pltpu.roll(e_hi, 4, 0)).astype(BF16)
            rpay[2 * zz + 1, :, 0:WIDTH] = g[8:16].astype(BF16)
            rpay[2 * zz + 1, :, WIDTH:] = jnp.where(low8, pltpu.roll(e_lo, 4, 0), e_hi).astype(BF16)
            if a == 0:
                z_copy(rpay, rrcv, bs, br, partner).start()
            else:
                for k in (0, 1):
                    z_copy(rpay, rrcv, bs, br, 2 * zz + k).start()
    own_ret = pltpu.make_async_copy(rpay.at[me], rrcv.at[me], lsem.at[3])
    own_ret.start()

    tok_t = iota((tokens, n), 0).astype(F32)
    dest = (tok_t >= starts) & (tok_t < ends)
    owner = jnp.sum(jnp.where(dest, iota((tokens, n), 1).astype(F32), 0.0), axis=1, keepdims=True)
    slot = jnp.sum(jnp.where(dest, tok_t - starts, 0.0), axis=1, keepdims=True)
    lane_p = iota((tokens, rows), 1)
    lane_i = lane_p & 7
    here = (lane_p // 8).astype(F32) == owner
    lane_f = lane_i.astype(F32)
    take_first = (here & (lane_f == slot)).astype(F32).astype(BF16)
    take_lo = (here & (lane_i < 4) & (lane_f + 8.0 == slot)).astype(F32).astype(BF16)
    take_hi = (here & (lane_i >= 4) & (lane_f + 4.0 == slot)).astype(F32).astype(BF16)

    own_ret.wait()
    weights[ncol + 1].wait()

    def ret_wait(o, carry):
        z_wait(rrcv, bs, br, lax.rem(me + o, n))
        return carry

    lax.fori_loop(1, n, ret_wait, 0)
    back = rrcv[:, :, 0:WIDTH].astype(F32).reshape(rows, WIDTH).astype(BF16)
    back_x = rrcv[:, :, WIDTH:].astype(F32).reshape(rows, WIDTH // 2).astype(BF16)
    gated = dot(take_first, back)
    gated_lo = gated[:, : WIDTH // 2] + dot(take_lo, back_x)
    gated_hi = gated[:, WIDTH // 2 :] + dot(take_hi, back_x)
    branch = dot(gated_lo.astype(BF16), wo[: WIDTH // 2]) + dot(gated_hi.astype(BF16), wo[WIDTH // 2 :])
    out[...] = (hidden.astype(F32) + branch.astype(BF16).astype(F32)).astype(BF16)

    for o in range(1, ncol):
        x_copy(o).wait_send()

    def drain(o, carry):
        peer = lax.rem(me + o, n)
        z_copy(sgp, sgr, gs, gr, peer).wait_send()
        copy(pay.at[peer], rcv.at[me], fs, fr, peer).wait_send()
        z_copy(rpay, rrcv, bs, br, peer).wait_send()
        return carry

    lax.fori_loop(1, n, drain, 0)


def on_device(n, ncol, lookups, input_weight, joined_weight, output_weight, owner_counts, user_index):
    tokens = user_index.shape[0]
    dma = pltpu.SemaphoreType.DMA
    anyspace = pl.BlockSpec(memory_space=pl.ANY)
    vmem = pl.BlockSpec(memory_space=pltpu.VMEM)
    return pl.pallas_call(
        functools.partial(kernel, n, ncol),
        name="hstu",
        out_shape=jax.ShapeDtypeStruct((tokens, D), BF16),
        in_specs=[anyspace, anyspace, anyspace, anyspace, vmem, vmem],
        out_specs=vmem,
        scratch_shapes=[
            pltpu.VMEM((ncol, tokens, D // ncol), BF16),
            pltpu.VMEM((D, D), BF16),
            pltpu.VMEM((D, 4 * WIDTH), BF16),
            pltpu.VMEM((WIDTH, D), BF16),
            pltpu.VMEM((n, ncol, 8, 3 * D // 2 // ncol), BF16),
            pltpu.VMEM((n, ncol, 8, 3 * D // 2 // ncol), BF16),
            pltpu.VMEM((n, 1, 128), F32),
            pltpu.VMEM((n, 1, 128), F32),
            pltpu.VMEM((n * CAP, 4 * WIDTH), BF16),
            pltpu.VMEM((n * CAP, 128), F32),
            pltpu.VMEM((n * CAP, WIDTH), F32),
            pltpu.VMEM((n, 8, 3 * WIDTH // 2), BF16),
            pltpu.VMEM((n, 8, 3 * WIDTH // 2), BF16),
            pltpu.SemaphoreType.REGULAR, pltpu.SemaphoreType.REGULAR, pltpu.SemaphoreType.REGULAR,
            dma((ncol + 2,)), dma((4,)), dma((ncol,)), dma((ncol,)),
            dma((n,)), dma((n,)), dma((n,)), dma((n,)), dma((n,)), dma((n,)),
        ],
        compiler_params=pltpu.CompilerParams(collective_id=0, has_side_effects=True),
    )(lookups, input_weight, joined_weight, output_weight, owner_counts, user_index.reshape(1, tokens))


def solution(mesh):
    return jax.shard_map(
        functools.partial(on_device, mesh.shape["batch"], mesh.shape["col"]),
        mesh=mesh,
        in_specs=(
            P(("rep", "batch"), "col"),
            P(),
            P(),
            P(),
            P(("rep", "batch", "col"), None),
            P(("rep", "batch", "col")),
        ),
        out_specs=P(("rep", "batch", "col"), None),
        check_vma=False,
    )
```

```python
import functools

import jax
import jax.numpy as jnp
from jax import lax
from jax.experimental import pallas as pl
from jax.experimental.pallas import tpu as pltpu
from jax.sharding import PartitionSpec as P

MESH = pl.DeviceIdType.MESH
HEADS = 4
HEAD_DIM = 128
WIDTH = HEADS * HEAD_DIM
D = 1024
CAP = 12
ROWS = 24
eps_norm = 1e-06
F32 = jnp.float32
BF16 = jnp.bfloat16

OFFSETS = [0, 8] + [s * o for o in range(7, 0, -1) for s in (1, -1)]
REL = (0, 1, 3, 2)
GROUPS = [(0, 6), (6, 10), (10, 16)]


def group_of(o):
    a = OFFSETS.index(abs(o))
    return [a0 <= a < a1 for a0, a1 in GROUPS].index(True)


def layer_norm(values):
    row_mean = jnp.mean(values, axis=-1, keepdims=True)
    centered = values - row_mean
    row_var = jnp.mean(centered * centered, axis=-1, keepdims=True)
    return centered * lax.rsqrt(row_var + eps_norm)


def silu(values, scale=1.0):
    half = values * (0.5 * scale)
    return half + half * jnp.tanh(half)


def dot(a, b):
    return jnp.dot(a, b, preferred_element_type=F32)


def dot_nt(a, b):
    return lax.dot_general(a, b, (((1,), (1,)), ((), ())), preferred_element_type=F32)


def iota(shape, dim):
    return lax.broadcasted_iota(jnp.int32, shape, dim)


def position(row, z, chips):
    a = row // ROWS
    i = row - a * ROWS
    step = jnp.where(a == 0, 0, chips // 2 - a // 2)
    off = jnp.where((a & 1) == 1, chips - step, step)
    zz = z + off
    zz = jnp.where(zz >= chips, zz - chips, zz)
    zz = jnp.where(zz >= chips, zz - chips, zz)
    second = jnp.where(i < 16, i // 8, (i - 16) // 4)
    slot = jnp.where(i < 16, i & 7, 8 + (i & 3))
    return (2 * zz + second) * CAP + slot


def kernel(
    n, ncol, lk, win_h, wj_h, wo_h, cnt_h, usr_h, out,
    cnt, usr, tok, win, wj, wo, pay, rcv, sgp, sgr, joined, umat, okm, mixed, rpay, rrcv,
    near2, near4, near8, wsem, lsem, xs, xr, gs, gr, fs, fr, bs, br,
):
    me = lax.axis_index("batch")
    col = lax.axis_index("col")
    chips = n // 2
    z, core = me // 2, lax.rem(me, 2)
    tokens = usr.shape[1]
    barrier = pltpu.get_barrier_semaphore()
    partner = 2 * z + 1 - core
    slab = D // ncol

    def at(o):
        return lax.rem(z + o + chips, chips)

    def signal(sem, peer):
        pl.semaphore_signal(sem, inc=1, device_id={"batch": peer}, device_id_type=MESH)

    for o in range(1, ncol):
        pl.semaphore_signal(barrier, inc=1, device_id={"col": lax.rem(col + o, ncol)}, device_id_type=MESH)
    signal(barrier, partner)
    for o in (1, -1):
        for k in (0, 1):
            signal(barrier, 2 * at(o) + k)

    small = [pltpu.make_async_copy(cnt_h, cnt, lsem.at[4]), pltpu.make_async_copy(usr_h, usr, lsem.at[5])]
    for c in small:
        c.start()
    own_tok = pltpu.make_async_copy(lk.at[pl.ds(col * tokens, tokens)], tok.at[0], lsem.at[0])
    own_tok.start()
    weights = [
        pltpu.make_async_copy(
            win_h.at[pl.ds(lax.rem(col + REL[j], ncol) * slab, slab)], win.at[pl.ds(j * slab, slab)], wsem.at[0]
        )
        for j in range(ncol)
    ]
    weights.append(pltpu.make_async_copy(wj_h, wj, wsem.at[1]))
    weights.append(pltpu.make_async_copy(wo_h, wo, wsem.at[2]))
    for w in weights:
        w.start()

    def x_copy(o):
        peer = lax.rem(col + o, ncol)
        j = REL.index(ncol - o)
        return pltpu.make_async_remote_copy(
            src_ref=lk.at[pl.ds(peer * tokens, tokens)], dst_ref=tok.at[j], send_sem=xs, recv_sem=xr,
            device_id={"col": peer}, device_id_type=MESH,
        )

    pl.semaphore_wait(barrier, ncol - 1 + 5)
    for o in (1, -1):
        signal(near2, 2 * at(o) + core)
    for o in range(1, ncol):
        x_copy(o).start()

    for c in small:
        c.wait()
    counts = cnt[...].astype(F32)
    upto = (iota((n, n), 0) <= iota((n, n), 1)).astype(F32).astype(BF16)
    ends = dot(jnp.broadcast_to(counts, (8, n)).astype(BF16), upto)[0:1]
    starts = ends - counts
    rows = 8 * n
    row_d, row_r = iota((rows, n), 0) // 8, iota((rows, 1), 0) & 7
    mine = row_d == iota((rows, n), 1)
    start_col = jnp.sum(jnp.where(mine, starts, 0.0), axis=1, keepdims=True)
    count_col = jnp.sum(jnp.where(mine, counts, 0.0), axis=1, keepdims=True)

    pl.semaphore_wait(near2, 2)
    for o in (2, -2):
        signal(near4, 2 * at(o) + core)

    lane_t = iota((rows, tokens), 1).astype(F32)
    first_r = row_r.astype(F32)
    last_r = 8.0 + (row_r & 3).astype(F32)
    want_first = jnp.where(first_r < count_col, start_col + first_r, -1.0)
    want_last = jnp.where(last_r < count_col, start_col + last_r, -1.0)
    is_first = lane_t == want_first
    is_last = lane_t == want_last
    pick_first = is_first.astype(F32).astype(BF16)
    pick_last = is_last.astype(F32).astype(BF16)

    def pack(j):
        first = dot(pick_first, tok[j])
        last = dot(pick_last, tok[j])
        fold = jnp.where(row_r < 4, last[:, : slab // 2], last[:, slab // 2 :])
        pay[:, j, :, 0:slab] = first.reshape(n, 8, slab).astype(BF16)
        pay[:, j, :, slab:] = fold.reshape(n, 8, slab // 2).astype(BF16)

    own_tok.wait()
    pack(0)

    def copy(src, dst, send, recv, peer):
        return pltpu.make_async_remote_copy(
            src_ref=src, dst_ref=dst, send_sem=send, recv_sem=recv, device_id={"batch": peer}, device_id_type=MESH
        )

    def whole(buf, blocks, send, recv):
        return copy(buf.at[pl.ds(0, blocks)], buf.at[pl.ds(0, blocks)], send, recv, partner)

    def send_own(peer, o):
        copy(pay.at[peer, pl.ds(0, 1)], rcv.at[me, pl.ds(0, 1)], fs, fr.at[group_of(o)], peer).start()

    def send_rest(peer, o):
        copy(pay.at[peer, pl.ds(1, ncol - 1)], rcv.at[me, pl.ds(1, ncol - 1)], fs, fr.at[group_of(o)], peer).start()

    def send_seg(peer, o):
        copy(sgp.at[peer], sgr.at[me], gs, gr, peer).start()

    def send_back(peer, o):
        copy(rpay.at[peer], rrcv.at[me], bs, br, peer).start()

    def send_ring(send, offsets):
        for o in offsets:
            for k in (0, 1):
                send(2 * at(o) + k, o)
                if 2 * o != chips:
                    send(2 * at(-o) + k, o)

    send_own(partner, 0)
    send_ring(send_own, [2, 1])
    pl.semaphore_wait(near4, 2)
    for o in (4, -4):
        signal(near8, 2 * at(o) + core)
    send_ring(send_own, [4, 3])

    users = usr[...].astype(F32) + 1.0
    seg_first = jnp.sum(jnp.where(is_first, users, 0.0), axis=1, keepdims=True)
    seg_last = jnp.sum(jnp.where(is_last, users, 0.0), axis=1, keepdims=True)
    lane = iota((rows, 128), 1)
    spread = jnp.where(lane == row_r, seg_first, 0.0) + jnp.where((lane == 8 + row_r) & (row_r < 4), seg_last, 0.0)
    own_rows = (iota((n, rows), 1) // 8 == iota((n, rows), 0)).astype(F32).astype(BF16)
    segs = dot(own_rows, spread.astype(BF16))
    for d in range(n):
        sgp[d] = segs[d : d + 1]

    pl.semaphore_wait(near8, 2)
    send_ring(send_own, [8, 7, 6, 5])
    send_seg(partner, 0)
    send_ring(send_seg, range(chips // 2, 0, -1))
    own_seg = pltpu.make_async_copy(sgp.at[me], sgr.at[me], lsem.at[1])
    own_seg.start()

    pltpu.make_async_remote_copy(
        src_ref=tok.at[pl.ds(1, ncol - 1)], dst_ref=tok.at[pl.ds(1, ncol - 1)], send_sem=xs, recv_sem=xr,
        device_id={"col": lax.rem(col + 1, ncol)}, device_id_type=MESH,
    ).wait_recv()
    for j in range(1, ncol):
        pack(j)
    send_rest(partner, 0)
    send_ring(send_rest, range(chips // 2, 0, -1))
    own_pay = pltpu.make_async_copy(pay.at[me], rcv.at[me], lsem.at[2])
    own_pay.start()

    pltpu.make_async_copy(win_h, win, wsem.at[0]).wait()
    hidden = dot(tok[0], win[0:slab])
    for j in range(1, ncol):
        hidden += dot(tok[j], win[j * slab : (j + 1) * slab])
    hidden = hidden.astype(BF16)

    low = iota((1, 8, 1), 1) < 4
    low8 = iota((8, 1), 0) < 4
    i24 = iota((ROWS, 128), 0)
    lane24 = iota((ROWS, 128), 1)
    want = jnp.where(i24 < 16, i24 & 7, 8 + (i24 & 3))
    is_a = (i24 < 8) | ((i24 >= 16) & (i24 < 20))
    own_seg.wait()
    whole(sgr, n - 1, gs, gr).wait_recv()
    for a in range(chips):
        zz = at(OFFSETS[a])
        seg = jnp.where(is_a, sgr[2 * zz], sgr[2 * zz + 1])
        seg = jnp.sum(jnp.where(lane24 == want, seg, 0.0), axis=1, keepdims=True)
        umat[a * ROWS : (a + 1) * ROWS, :] = jnp.where((lane24.astype(F32) == seg) & (lane24 > 0), 1.0, 0.0)
    slots = n * CAP
    users_all = umat[...].astype(BF16)
    pos_j = position(iota((1, slots), 1), z, chips)
    for a in range(0, chips, 4):
        part = slice(a * ROWS, (a + 4) * ROWS)
        pos_i = position(iota((4 * ROWS, 1), 0) + a * ROWS, z, chips)
        same = dot_nt(umat[part, :].astype(BF16), users_all) > 0.5
        okm[part, :] = jnp.where(same & (pos_j <= pos_i), 1.0, 0.0)

    weights[ncol].wait()
    own_pay.wait()
    for g, (a0, a1) in enumerate(GROUPS):
        whole(rcv, 2 * (a1 - a0) - (a0 == 0), fs, fr.at[g]).wait_recv()
        parts = []
        for a in range(a0, a1):
            zz = at(OFFSETS[a])
            va, vb = rcv[2 * zz].astype(F32), rcv[2 * zz + 1].astype(F32)
            ea, eb = va[:, :, slab:], vb[:, :, slab:]
            ex_lo = jnp.where(low, ea, pltpu.roll(eb, 4, 1))
            ex_hi = jnp.where(low, pltpu.roll(ea, 4, 1), eb)
            parts.append(jnp.concatenate([v[:, :, :slab] for v in (va, vb)] + [jnp.concatenate([ex_lo, ex_hi], axis=2)], axis=1))
        r0, r1 = a0 * ROWS, a1 * ROWS
        looked = jnp.concatenate(parts, axis=1).astype(BF16)
        projected = dot(looked[0], win[0:slab])
        for j in range(1, ncol):
            projected += dot(looked[j], win[j * slab : (j + 1) * slab])
        normed = layer_norm(projected.astype(BF16).astype(F32)).astype(BF16)

        def project(c, carry, normed=normed, r0=r0, r1=r1):
            cols = pl.ds(pl.multiple_of(c * WIDTH, WIDTH), WIDTH)
            joined[r0:r1, cols] = silu(dot(normed, wj[:, cols])).astype(BF16)
            return carry

        lax.fori_loop(0, 4, project, 0)

        for h in range(HEADS):
            vs = slice(WIDTH + h * HEAD_DIM, WIDTH + (h + 1) * HEAD_DIM)
            qs = slice(2 * WIDTH + h * HEAD_DIM, 2 * WIDTH + (h + 1) * HEAD_DIM)
            ks = slice(3 * WIDTH + h * HEAD_DIM, 3 * WIDTH + (h + 1) * HEAD_DIM)
            hs = slice(h * HEAD_DIM, (h + 1) * HEAD_DIM)
            w = silu(dot_nt(joined[0:r1, qs], joined[r0:r1, ks]), HEAD_DIM ** (-0.5))
            add = dot((w * okm[0:r1, r0:r1]).astype(BF16), joined[r0:r1, vs])
            if r0:
                mixed[0:r0, hs] += add[:r0]
                w = silu(dot_nt(joined[r0:r1, qs], joined[0:r0, ks]), HEAD_DIM ** (-0.5))
                mixed[r0:r1, hs] = add[r0:] + dot((w * okm[r0:r1, 0:r0]).astype(BF16), joined[0:r0, vs])
            else:
                mixed[0:r1, hs] = add

    for a0 in range(0, chips, 2):
        gated = layer_norm(mixed[a0 * ROWS : (a0 + 2) * ROWS, :]) * joined[a0 * ROWS : (a0 + 2) * ROWS, 0:WIDTH].astype(F32)
        for a in (a0 + 1, a0):
            zz = at(OFFSETS[a])
            g = gated[(a - a0) * ROWS : (a - a0 + 1) * ROWS]
            e_lo, e_hi = g[16:24, : WIDTH // 2], g[16:24, WIDTH // 2 :]
            rpay[2 * zz, :, 0:WIDTH] = g[0:8].astype(BF16)
            rpay[2 * zz, :, WIDTH:] = jnp.where(low8, e_lo, pltpu.roll(e_hi, 4, 0)).astype(BF16)
            rpay[2 * zz + 1, :, 0:WIDTH] = g[8:16].astype(BF16)
            rpay[2 * zz + 1, :, WIDTH:] = jnp.where(low8, pltpu.roll(e_lo, 4, 0), e_hi).astype(BF16)
            if a == 0:
                send_back(partner, 0)
            else:
                for k in (0, 1):
                    send_back(2 * zz + k, OFFSETS[a])
    own_ret = pltpu.make_async_copy(rpay.at[me], rrcv.at[me], lsem.at[3])
    own_ret.start()

    tok_t = iota((tokens, n), 0).astype(F32)
    dest = (tok_t >= starts) & (tok_t < ends)
    owner = jnp.sum(jnp.where(dest, iota((tokens, n), 1).astype(F32), 0.0), axis=1, keepdims=True)
    slot = jnp.sum(jnp.where(dest, tok_t - starts, 0.0), axis=1, keepdims=True)
    lane_p = iota((tokens, rows), 1)
    lane_i = lane_p & 7
    here = (lane_p // 8).astype(F32) == owner
    lane_f = lane_i.astype(F32)
    take_first = (here & (lane_f == slot)).astype(F32).astype(BF16)
    take_lo = (here & (lane_i < 4) & (lane_f + 8.0 == slot)).astype(F32).astype(BF16)
    take_hi = (here & (lane_i >= 4) & (lane_f + 4.0 == slot)).astype(F32).astype(BF16)

    pltpu.make_async_remote_copy(
        src_ref=tok.at[pl.ds(1, ncol - 1)], dst_ref=tok.at[pl.ds(1, ncol - 1)], send_sem=xs, recv_sem=xr,
        device_id={"col": lax.rem(col + 1, ncol)}, device_id_type=MESH,
    ).wait_send()
    whole(sgp, n - 1, gs, gr).wait_send()
    whole(pay, n - 1, fs, fr.at[0]).wait_send()
    own_ret.wait()
    weights[ncol + 1].wait()

    whole(rrcv, n - 1, bs, br).wait_recv()
    back = rrcv[:, :, 0:WIDTH].astype(F32).reshape(rows, WIDTH).astype(BF16)
    back_x = rrcv[:, :, WIDTH:].astype(F32).reshape(rows, WIDTH // 2).astype(BF16)
    gated = dot(take_first, back)
    gated_lo = gated[:, : WIDTH // 2] + dot(take_lo, back_x)
    gated_hi = gated[:, WIDTH // 2 :] + dot(take_hi, back_x)
    branch = dot(gated_lo.astype(BF16), wo[: WIDTH // 2]) + dot(gated_hi.astype(BF16), wo[WIDTH // 2 :])
    out[...] = (hidden.astype(F32) + branch.astype(BF16).astype(F32)).astype(BF16)

    whole(rpay, n - 1, bs, br).wait_send()


def on_device(n, ncol, lookups, input_weight, joined_weight, output_weight, owner_counts, user_index):
    tokens = user_index.shape[0]
    dma = pltpu.SemaphoreType.DMA
    anyspace = pl.BlockSpec(memory_space=pl.ANY)
    vmem = pl.BlockSpec(memory_space=pltpu.VMEM)
    return pl.pallas_call(
        functools.partial(kernel, n, ncol),
        name="hstu",
        out_shape=pltpu.VMEM((tokens, D), BF16),
        in_specs=[anyspace] * 6,
        out_specs=vmem,
        scratch_shapes=[
            pltpu.VMEM((1, n), jnp.int32),
            pltpu.VMEM((1, tokens), jnp.int32),
            pltpu.VMEM((ncol, tokens, D // ncol), BF16),
            pltpu.VMEM((D, D), BF16),
            pltpu.VMEM((D, 4 * WIDTH), BF16),
            pltpu.VMEM((WIDTH, D), BF16),
            pltpu.VMEM((n, ncol, 8, 3 * D // 2 // ncol), BF16),
            pltpu.VMEM((n, ncol, 8, 3 * D // 2 // ncol), BF16),
            pltpu.VMEM((n, 1, 128), F32),
            pltpu.VMEM((n, 1, 128), F32),
            pltpu.VMEM((n * CAP, 4 * WIDTH), BF16),
            pltpu.VMEM((n * CAP, 128), F32),
            pltpu.VMEM((n * CAP, n * CAP), F32),
            pltpu.VMEM((n * CAP, WIDTH), F32),
            pltpu.VMEM((n, 8, 3 * WIDTH // 2), BF16),
            pltpu.VMEM((n, 8, 3 * WIDTH // 2), BF16),
            pltpu.SemaphoreType.REGULAR, pltpu.SemaphoreType.REGULAR, pltpu.SemaphoreType.REGULAR,
            dma((3,)), dma((6,)), dma, dma, dma, dma, dma, dma((len(GROUPS),)), dma, dma,
        ],
        compiler_params=pltpu.CompilerParams(collective_id=0, has_side_effects=True),
    )(lookups, input_weight, joined_weight, output_weight, owner_counts, user_index.reshape(1, tokens))


def solution(mesh):
    return jax.shard_map(
        functools.partial(on_device, mesh.shape["batch"], mesh.shape["col"]),
        mesh=mesh,
        in_specs=(
            P(("rep", "batch"), "col"),
            P(),
            P(),
            P(),
            P(("rep", "batch", "col"), None),
            P(("rep", "batch", "col")),
        ),
        out_specs=P(("rep", "batch", "col"), None),
        check_vma=False,
    )
```

```python
import functools

import jax
import jax.numpy as jnp
from jax import lax
from jax.experimental import pallas as pl
from jax.experimental.pallas import tpu as pltpu
from jax.sharding import PartitionSpec as P

MESH = pl.DeviceIdType.MESH
HEADS = 4
HEAD_DIM = 128
WIDTH = HEADS * HEAD_DIM
D = 1024
CAP = 12
ROWS = 24
eps_norm = 1e-06
F32 = jnp.float32
BF16 = jnp.bfloat16

OFFSETS = [0, 8] + [s * o for o in range(7, 0, -1) for s in (1, -1)]
REL = (0, 1, 3, 2)
GROUPS = [(0, 6), (6, 10), (10, 16)]


def group_of(o):
    a = OFFSETS.index(abs(o))
    return [a0 <= a < a1 for a0, a1 in GROUPS].index(True)


def layer_norm(values):
    row_mean = jnp.mean(values, axis=-1, keepdims=True)
    centered = values - row_mean
    row_var = jnp.mean(centered * centered, axis=-1, keepdims=True)
    return centered * lax.rsqrt(row_var + eps_norm)


def silu(values, scale=1.0):
    half = values * (0.5 * scale)
    return half + half * jnp.tanh(half)


def dot(a, b):
    return jnp.dot(a, b, preferred_element_type=F32)


def dot_nt(a, b):
    return lax.dot_general(a, b, (((1,), (1,)), ((), ())), preferred_element_type=F32)


def iota(shape, dim):
    return lax.broadcasted_iota(jnp.int32, shape, dim)


def position(row, z, chips):
    a = row // ROWS
    i = row - a * ROWS
    step = jnp.where(a == 0, 0, chips // 2 - a // 2)
    off = jnp.where((a & 1) == 1, chips - step, step)
    zz = z + off
    zz = jnp.where(zz >= chips, zz - chips, zz)
    zz = jnp.where(zz >= chips, zz - chips, zz)
    second = jnp.where(i < 16, i // 8, (i - 16) // 4)
    slot = jnp.where(i < 16, i & 7, 8 + (i & 3))
    return (2 * zz + second) * CAP + slot


def kernel(
    n, ncol, lk, win_h, wj_h, wo_h, cnt_h, usr_h, out,
    cnt, usr, tok, win, wj, wo, pay, rcv, sgp, sgr, joined, umat, okm, mixed, rpay, rrcv,
    wsem, lsem, xs, xr, gs, gr, fs, fr, bs, br,
):
    me = lax.axis_index("batch")
    col = lax.axis_index("col")
    chips = n // 2
    z, core = me // 2, lax.rem(me, 2)
    tokens = usr.shape[1]
    barrier = pltpu.get_barrier_semaphore()
    partner = 2 * z + 1 - core
    slab = D // ncol

    def at(o):
        return lax.rem(z + o + chips, chips)

    def signal(sem, peer):
        pl.semaphore_signal(sem, inc=1, device_id={"batch": peer}, device_id_type=MESH)

    small = [pltpu.make_async_copy(cnt_h, cnt, lsem.at[4]), pltpu.make_async_copy(usr_h, usr, lsem.at[5])]
    for c in small:
        c.start()
    own_tok = pltpu.make_async_copy(lk.at[pl.ds(col * tokens, tokens)], tok.at[0], lsem.at[0])
    own_tok.start()
    def greet(i, carry):
        o = chips // 2 - i
        for k in (0, 1):
            signal(barrier, 2 * at(o) + k)
            signal(barrier, 2 * at(-o) + k)
        return carry

    for k in (0, 1):
        signal(barrier, 2 * at(chips // 2) + k)
    lax.fori_loop(1, chips // 2, greet, 0)
    for o in range(1, ncol):
        pl.semaphore_signal(barrier, inc=1, device_id={"col": lax.rem(col + o, ncol)}, device_id_type=MESH)
    signal(barrier, partner)

    weights = [
        pltpu.make_async_copy(
            win_h.at[pl.ds(lax.rem(col + REL[j], ncol) * slab, slab)], win.at[pl.ds(j * slab, slab)], wsem.at[0]
        )
        for j in range(ncol)
    ]
    weights.append(pltpu.make_async_copy(wj_h, wj, wsem.at[1]))
    weights.append(pltpu.make_async_copy(wo_h, wo, wsem.at[2]))
    for w in weights:
        w.start()

    def x_copy(o):
        peer = lax.rem(col + o, ncol)
        j = REL.index(ncol - o)
        return pltpu.make_async_remote_copy(
            src_ref=lk.at[pl.ds(peer * tokens, tokens)], dst_ref=tok.at[j], send_sem=xs, recv_sem=xr.at[j // 3],
            device_id={"col": peer}, device_id_type=MESH,
        )

    for c in small:
        c.wait()
    counts = cnt[...].astype(F32)
    upto = (iota((n, n), 0) <= iota((n, n), 1)).astype(F32).astype(BF16)
    ends = dot(jnp.broadcast_to(counts, (8, n)).astype(BF16), upto)[0:1]
    starts = ends - counts
    rows = 8 * n
    row_d, row_r = iota((rows, n), 0) // 8, iota((rows, 1), 0) & 7
    mine = row_d == iota((rows, n), 1)
    start_col = jnp.sum(jnp.where(mine, starts, 0.0), axis=1, keepdims=True)
    count_col = jnp.sum(jnp.where(mine, counts, 0.0), axis=1, keepdims=True)

    lane_t = iota((rows, tokens), 1).astype(F32)
    first_r = row_r.astype(F32)
    last_r = 8.0 + (row_r & 3).astype(F32)
    want_first = jnp.where(first_r < count_col, start_col + first_r, -1.0)
    want_last = jnp.where(last_r < count_col, start_col + last_r, -1.0)
    is_first = lane_t == want_first
    is_last = lane_t == want_last
    pick_first = is_first.astype(F32).astype(BF16)
    pick_last = is_last.astype(F32).astype(BF16)

    def pack(j):
        first = dot(pick_first, tok[j])
        last = dot(pick_last, tok[j])
        fold = jnp.where(row_r < 4, last[:, : slab // 2], last[:, slab // 2 :])
        pay[:, j, :, 0:slab] = first.reshape(n, 8, slab).astype(BF16)
        pay[:, j, :, slab:] = fold.reshape(n, 8, slab // 2).astype(BF16)

    own_tok.wait()
    pack(0)

    def copy(src, dst, send, recv, peer):
        return pltpu.make_async_remote_copy(
            src_ref=src, dst_ref=dst, send_sem=send, recv_sem=recv, device_id={"batch": peer}, device_id_type=MESH
        )

    def whole(buf, blocks, send, recv):
        return copy(buf.at[pl.ds(0, blocks)], buf.at[pl.ds(0, blocks)], send, recv, partner)

    def send_cols(j0, j1, peer, o):
        cols = pl.ds(j0, j1 - j0)
        copy(pay.at[peer, cols], rcv.at[me, cols], fs, fr.at[group_of(o)], peer).start()

    def send_seg(peer, o):
        copy(sgp.at[peer], sgr.at[me], gs, gr, peer).start()

    def send_back(peer, o):
        copy(rpay.at[peer], rrcv.at[me], bs, br, peer).start()

    def send_ring(send, offsets):
        for o in offsets:
            for k in (0, 1):
                send(2 * at(o) + k, o)
                if 2 * o != chips:
                    send(2 * at(-o) + k, o)

    pl.semaphore_wait(barrier, n - 1 + ncol - 1)
    for o in (1, 3, 2):
        x_copy(o).start()

    send_cols(0, 1, partner, 0)
    send_ring(functools.partial(send_cols, 0, 1), range(chips // 2, 0, -1))
    users = usr[...].astype(F32) + 1.0
    seg_first = jnp.sum(jnp.where(is_first, users, 0.0), axis=1, keepdims=True)
    seg_last = jnp.sum(jnp.where(is_last, users, 0.0), axis=1, keepdims=True)
    lane = iota((rows, 128), 1)
    spread = jnp.where(lane == row_r, seg_first, 0.0) + jnp.where((lane == 8 + row_r) & (row_r < 4), seg_last, 0.0)
    own_rows = (iota((n, rows), 1) // 8 == iota((n, rows), 0)).astype(F32).astype(BF16)
    segs = dot(own_rows, spread.astype(BF16))
    for d in range(n):
        sgp[d] = segs[d : d + 1]

    send_seg(partner, 0)
    send_ring(send_seg, range(chips // 2, 0, -1))
    own_seg = pltpu.make_async_copy(sgp.at[me], sgr.at[me], lsem.at[1])
    own_seg.start()

    def x_whole(j0, j1, recv):
        part = tok.at[pl.ds(j0, j1 - j0)]
        return pltpu.make_async_remote_copy(
            src_ref=part, dst_ref=part, send_sem=xs, recv_sem=recv,
            device_id={"col": lax.rem(col + 1, ncol)}, device_id_type=MESH,
        )

    x_whole(1, 3, xr.at[0]).wait_recv()
    pack(1)
    pack(2)
    send_ring(functools.partial(send_cols, 1, 3), [8, 7])
    x_whole(3, 4, xr.at[1]).wait_recv()
    pack(3)
    send_ring(functools.partial(send_cols, 3, 4), [8, 7])
    send_cols(1, 4, partner, 0)
    send_ring(functools.partial(send_cols, 1, 4), range(chips // 2 - 2, 0, -1))
    own_pay = pltpu.make_async_copy(pay.at[me], rcv.at[me], lsem.at[2])
    own_pay.start()

    pltpu.make_async_copy(win_h, win, wsem.at[0]).wait()
    hidden = dot(tok[0], win[0:slab])
    for j in range(1, ncol):
        hidden += dot(tok[j], win[j * slab : (j + 1) * slab])
    hidden = hidden.astype(BF16)

    low = iota((1, 8, 1), 1) < 4
    low8 = iota((8, 1), 0) < 4
    i24 = iota((ROWS, 128), 0)
    lane24 = iota((ROWS, 128), 1)
    want = jnp.where(i24 < 16, i24 & 7, 8 + (i24 & 3))
    is_a = (i24 < 8) | ((i24 >= 16) & (i24 < 20))
    own_seg.wait()
    whole(sgr, n - 1, gs, gr).wait_recv()
    for a in range(chips):
        zz = at(OFFSETS[a])
        seg = jnp.where(is_a, sgr[2 * zz], sgr[2 * zz + 1])
        seg = jnp.sum(jnp.where(lane24 == want, seg, 0.0), axis=1, keepdims=True)
        umat[a * ROWS : (a + 1) * ROWS, :] = jnp.where((lane24.astype(F32) == seg) & (lane24 > 0), 1.0, 0.0)
    slots = n * CAP
    users_all = umat[...].astype(BF16)
    pos_j = position(iota((1, slots), 1), z, chips)
    for a in range(0, chips, 4):
        part = slice(a * ROWS, (a + 4) * ROWS)
        pos_i = position(iota((4 * ROWS, 1), 0) + a * ROWS, z, chips)
        same = dot_nt(umat[part, :].astype(BF16), users_all) > 0.5
        okm[part, :] = jnp.where(same & (pos_j <= pos_i), 1.0, 0.0)

    weights[ncol].wait()
    own_pay.wait()
    for g, (a0, a1) in enumerate(GROUPS):
        whole(rcv, 2 * (a1 - a0) - (a0 == 0), fs, fr.at[g]).wait_recv()
        parts = []
        for a in range(a0, a1):
            zz = at(OFFSETS[a])
            va, vb = rcv[2 * zz].astype(F32), rcv[2 * zz + 1].astype(F32)
            ea, eb = va[:, :, slab:], vb[:, :, slab:]
            ex_lo = jnp.where(low, ea, pltpu.roll(eb, 4, 1))
            ex_hi = jnp.where(low, pltpu.roll(ea, 4, 1), eb)
            parts.append(jnp.concatenate([v[:, :, :slab] for v in (va, vb)] + [jnp.concatenate([ex_lo, ex_hi], axis=2)], axis=1))
        r0, r1 = a0 * ROWS, a1 * ROWS
        looked = jnp.concatenate(parts, axis=1).astype(BF16)
        projected = dot(looked[0], win[0:slab])
        for j in range(1, ncol):
            projected += dot(looked[j], win[j * slab : (j + 1) * slab])
        normed = layer_norm(projected.astype(BF16).astype(F32)).astype(BF16)

        def project(c0, c1, normed=normed, r0=r0, r1=r1):
            joined[r0:r1, c0:c1] = silu(dot(normed, wj[:, c0:c1])).astype(BF16)

        for c in (3, 2, 1):
            project(c * WIDTH, (c + 1) * WIDTH)

        for h in range(HEADS):
            vs = slice(WIDTH + h * HEAD_DIM, WIDTH + (h + 1) * HEAD_DIM)
            qs = slice(2 * WIDTH + h * HEAD_DIM, 2 * WIDTH + (h + 1) * HEAD_DIM)
            ks = slice(3 * WIDTH + h * HEAD_DIM, 3 * WIDTH + (h + 1) * HEAD_DIM)
            hs = slice(h * HEAD_DIM, (h + 1) * HEAD_DIM)
            w = silu(dot_nt(joined[0:r1, qs], joined[r0:r1, ks]), HEAD_DIM ** (-0.5))
            add = dot((w * okm[0:r1, r0:r1]).astype(BF16), joined[r0:r1, vs])
            if r0:
                mixed[0:r0, hs] += add[:r0]
                w = silu(dot_nt(joined[r0:r1, qs], joined[0:r0, ks]), HEAD_DIM ** (-0.5))
                mixed[r0:r1, hs] = add[r0:] + dot((w * okm[r0:r1, 0:r0]).astype(BF16), joined[0:r0, vs])
            else:
                mixed[0:r1, hs] = add
            if h % 2 == 0:
                project(h * HEAD_DIM, (h + 2) * HEAD_DIM)

    for a0 in range(0, chips, 2):
        gated = layer_norm(mixed[a0 * ROWS : (a0 + 2) * ROWS, :]) * joined[a0 * ROWS : (a0 + 2) * ROWS, 0:WIDTH].astype(F32)
        for a in (a0 + 1, a0):
            zz = at(OFFSETS[a])
            g = gated[(a - a0) * ROWS : (a - a0 + 1) * ROWS]
            e_lo, e_hi = g[16:24, : WIDTH // 2], g[16:24, WIDTH // 2 :]
            rpay[2 * zz, :, 0:WIDTH] = g[0:8].astype(BF16)
            rpay[2 * zz, :, WIDTH:] = jnp.where(low8, e_lo, pltpu.roll(e_hi, 4, 0)).astype(BF16)
            rpay[2 * zz + 1, :, 0:WIDTH] = g[8:16].astype(BF16)
            rpay[2 * zz + 1, :, WIDTH:] = jnp.where(low8, pltpu.roll(e_lo, 4, 0), e_hi).astype(BF16)
            if a == 0:
                send_back(partner, 0)
            else:
                for k in (0, 1):
                    send_back(2 * zz + k, OFFSETS[a])
    own_ret = pltpu.make_async_copy(rpay.at[me], rrcv.at[me], lsem.at[3])
    own_ret.start()

    tok_t = iota((tokens, n), 0).astype(F32)
    dest = (tok_t >= starts) & (tok_t < ends)
    owner = jnp.sum(jnp.where(dest, iota((tokens, n), 1).astype(F32), 0.0), axis=1, keepdims=True)
    slot = jnp.sum(jnp.where(dest, tok_t - starts, 0.0), axis=1, keepdims=True)
    lane_p = iota((tokens, rows), 1)
    lane_i = lane_p & 7
    here = (lane_p // 8).astype(F32) == owner
    lane_f = lane_i.astype(F32)
    take_first = (here & (lane_f == slot)).astype(F32).astype(BF16)
    take_lo = (here & (lane_i < 4) & (lane_f + 8.0 == slot)).astype(F32).astype(BF16)
    take_hi = (here & (lane_i >= 4) & (lane_f + 4.0 == slot)).astype(F32).astype(BF16)

    x_whole(1, ncol, xr.at[0]).wait_send()
    whole(sgp, n - 1, gs, gr).wait_send()
    whole(pay, n - 1, fs, fr.at[0]).wait_send()
    own_ret.wait()
    weights[ncol + 1].wait()

    whole(rrcv, n - 1, bs, br).wait_recv()
    back = rrcv[:, :, 0:WIDTH].astype(F32).reshape(rows, WIDTH).astype(BF16)
    back_x = rrcv[:, :, WIDTH:].astype(F32).reshape(rows, WIDTH // 2).astype(BF16)
    gated = dot(take_first, back)
    gated_lo = gated[:, : WIDTH // 2] + dot(take_lo, back_x)
    gated_hi = gated[:, WIDTH // 2 :] + dot(take_hi, back_x)
    branch = dot(gated_lo.astype(BF16), wo[: WIDTH // 2]) + dot(gated_hi.astype(BF16), wo[WIDTH // 2 :])
    out[...] = (hidden.astype(F32) + branch.astype(BF16).astype(F32)).astype(BF16)

    whole(rpay, n - 1, bs, br).wait_send()


def on_device(n, ncol, lookups, input_weight, joined_weight, output_weight, owner_counts, user_index):
    tokens = user_index.shape[0]
    dma = pltpu.SemaphoreType.DMA
    anyspace = pl.BlockSpec(memory_space=pl.ANY)
    vmem = pl.BlockSpec(memory_space=pltpu.VMEM)
    return pl.pallas_call(
        functools.partial(kernel, n, ncol),
        name="hstu",
        out_shape=pltpu.VMEM((tokens, D), BF16),
        in_specs=[anyspace] * 6,
        out_specs=vmem,
        scratch_shapes=[
            pltpu.VMEM((1, n), jnp.int32),
            pltpu.VMEM((1, tokens), jnp.int32),
            pltpu.VMEM((ncol, tokens, D // ncol), BF16),
            pltpu.VMEM((D, D), BF16),
            pltpu.VMEM((D, 4 * WIDTH), BF16),
            pltpu.VMEM((WIDTH, D), BF16),
            pltpu.VMEM((n, ncol, 8, 3 * D // 2 // ncol), BF16),
            pltpu.VMEM((n, ncol, 8, 3 * D // 2 // ncol), BF16),
            pltpu.VMEM((n, 1, 128), F32),
            pltpu.VMEM((n, 1, 128), F32),
            pltpu.VMEM((n * CAP, 4 * WIDTH), BF16),
            pltpu.VMEM((n * CAP, 128), F32),
            pltpu.VMEM((n * CAP, n * CAP), F32),
            pltpu.VMEM((n * CAP, WIDTH), F32),
            pltpu.VMEM((n, 8, 3 * WIDTH // 2), BF16),
            pltpu.VMEM((n, 8, 3 * WIDTH // 2), BF16),
            dma((3,)), dma((6,)), dma, dma((2,)), dma, dma, dma, dma((len(GROUPS),)), dma, dma,
        ],
        compiler_params=pltpu.CompilerParams(collective_id=0, has_side_effects=True),
    )(lookups, input_weight, joined_weight, output_weight, owner_counts, user_index.reshape(1, tokens))


def solution(mesh):
    return jax.shard_map(
        functools.partial(on_device, mesh.shape["batch"], mesh.shape["col"]),
        mesh=mesh,
        in_specs=(
            P(("rep", "batch"), "col"),
            P(),
            P(),
            P(),
            P(("rep", "batch", "col"), None),
            P(("rep", "batch", "col")),
        ),
        out_specs=P(("rep", "batch", "col"), None),
        check_vma=False,
    )
```

```python
import functools

import jax
import jax.numpy as jnp
from jax import lax
from jax.experimental import pallas as pl
from jax.experimental.pallas import tpu as pltpu
from jax.sharding import PartitionSpec as P

MESH = pl.DeviceIdType.MESH
HEADS = 4
HEAD_DIM = 128
WIDTH = HEADS * HEAD_DIM
D = 1024
CAP = 12
ROWS = 24
eps_norm = 1e-06
F32 = jnp.float32
BF16 = jnp.bfloat16

OFFSETS = [0, 8] + [s * o for o in range(7, 0, -1) for s in (1, -1)]
REL = (0, 1, 3, 2)
GROUPS = [(0, 6), (6, 10), (10, 16)]


def group_of(o):
    a = OFFSETS.index(abs(o))
    return [a0 <= a < a1 for a0, a1 in GROUPS].index(True)


def layer_norm(values):
    row_mean = jnp.mean(values, axis=-1, keepdims=True)
    centered = values - row_mean
    row_var = jnp.mean(centered * centered, axis=-1, keepdims=True)
    return centered * lax.rsqrt(row_var + eps_norm)


def silu(values, scale=1.0):
    half = values * (0.5 * scale)
    return half + half * jnp.tanh(half)


def dot(a, b):
    return jnp.dot(a, b, preferred_element_type=F32)


def dot_nt(a, b):
    return lax.dot_general(a, b, (((1,), (1,)), ((), ())), preferred_element_type=F32)


def iota(shape, dim):
    return lax.broadcasted_iota(jnp.int32, shape, dim)


def position(row, z, chips):
    a = row // ROWS
    i = row - a * ROWS
    step = jnp.where(a == 0, 0, chips // 2 - a // 2)
    off = jnp.where((a & 1) == 1, chips - step, step)
    zz = z + off
    zz = jnp.where(zz >= chips, zz - chips, zz)
    zz = jnp.where(zz >= chips, zz - chips, zz)
    second = jnp.where(i < 16, i // 8, (i - 16) // 4)
    slot = jnp.where(i < 16, i & 7, 8 + (i & 3))
    return (2 * zz + second) * CAP + slot


def kernel(
    n, ncol, lk, win_h, wj_h, wo_h, cnt_h, usr_h, out,
    cnt, usr, tok, win, wj, wo, pay, rcv, sgp, sgr, joined, umat, okm, mixed, rpay, rrcv,
    wsem, lsem, xs, xr, gs, gr, fs, fr, bs, br,
):
    me = lax.axis_index("batch")
    col = lax.axis_index("col")
    chips = n // 2
    z, core = me // 2, lax.rem(me, 2)
    tokens = usr.shape[1]
    barrier = pltpu.get_barrier_semaphore()
    partner = 2 * z + 1 - core
    slab = D // ncol

    def at(o):
        return lax.rem(z + o + chips, chips)

    def signal(sem, peer):
        pl.semaphore_signal(sem, inc=1, device_id={"batch": peer}, device_id_type=MESH)

    small = [pltpu.make_async_copy(cnt_h, cnt, lsem.at[4]), pltpu.make_async_copy(usr_h, usr, lsem.at[5])]
    for c in small:
        c.start()
    own_tok = pltpu.make_async_copy(lk.at[pl.ds(col * tokens, tokens)], tok.at[0], lsem.at[0])
    own_tok.start()
    def greet(i, carry):
        o = chips // 2 - i
        for k in (0, 1):
            signal(barrier, 2 * at(o) + k)
            signal(barrier, 2 * at(-o) + k)
        return carry

    for k in (0, 1):
        signal(barrier, 2 * at(chips // 2) + k)
    lax.fori_loop(1, chips // 2, greet, 0)
    for o in range(1, ncol):
        pl.semaphore_signal(barrier, inc=1, device_id={"col": lax.rem(col + o, ncol)}, device_id_type=MESH)
    signal(barrier, partner)

    weights = [
        pltpu.make_async_copy(
            win_h.at[pl.ds(lax.rem(col + REL[j], ncol) * slab, slab)], win.at[pl.ds(j * slab, slab)], wsem.at[0]
        )
        for j in range(ncol)
    ]
    weights.append(pltpu.make_async_copy(wj_h, wj, wsem.at[1]))
    weights.append(pltpu.make_async_copy(wo_h, wo, wsem.at[2]))
    for w in weights:
        w.start()

    def x_copy(o):
        peer = lax.rem(col + o, ncol)
        j = REL.index(ncol - o)
        return pltpu.make_async_remote_copy(
            src_ref=lk.at[pl.ds(peer * tokens, tokens)], dst_ref=tok.at[j], send_sem=xs, recv_sem=xr.at[j // 3],
            device_id={"col": peer}, device_id_type=MESH,
        )

    for c in small:
        c.wait()
    counts = cnt[...].astype(F32)
    upto = (iota((n, n), 0) <= iota((n, n), 1)).astype(F32).astype(BF16)
    ends = dot(jnp.broadcast_to(counts, (8, n)).astype(BF16), upto)[0:1]
    starts = ends - counts
    rows = 8 * n
    row_d, row_r = iota((rows, n), 0) // 8, iota((rows, 1), 0) & 7
    mine = row_d == iota((rows, n), 1)
    start_col = jnp.sum(jnp.where(mine, starts, 0.0), axis=1, keepdims=True)
    count_col = jnp.sum(jnp.where(mine, counts, 0.0), axis=1, keepdims=True)

    lane_t = iota((rows, tokens), 1).astype(F32)
    first_r = row_r.astype(F32)
    last_r = 8.0 + (row_r & 3).astype(F32)
    want_first = jnp.where(first_r < count_col, start_col + first_r, -1.0)
    want_last = jnp.where(last_r < count_col, start_col + last_r, -1.0)
    is_first = lane_t == want_first
    is_last = lane_t == want_last
    pick_first = is_first.astype(F32).astype(BF16)
    pick_last = is_last.astype(F32).astype(BF16)

    def pack(j):
        first = dot(pick_first, tok[j])
        last = dot(pick_last, tok[j])
        fold = jnp.where(row_r < 4, last[:, : slab // 2], last[:, slab // 2 :])
        pay[:, j, :, 0:slab] = first.reshape(n, 8, slab).astype(BF16)
        pay[:, j, :, slab:] = fold.reshape(n, 8, slab // 2).astype(BF16)

    own_tok.wait()
    pack(0)

    def copy(src, dst, send, recv, peer):
        return pltpu.make_async_remote_copy(
            src_ref=src, dst_ref=dst, send_sem=send, recv_sem=recv, device_id={"batch": peer}, device_id_type=MESH
        )

    def whole(buf, blocks, send, recv):
        return copy(buf.at[pl.ds(0, blocks)], buf.at[pl.ds(0, blocks)], send, recv, partner)

    def send_cols(j0, j1, peer, o):
        cols = pl.ds(j0, j1 - j0)
        copy(pay.at[peer, cols], rcv.at[me, cols], fs, fr.at[group_of(o)], peer).start()

    def send_seg(peer, o):
        copy(sgp.at[peer], sgr.at[me], gs, gr, peer).start()

    def send_back(peer, o):
        copy(rpay.at[peer], rrcv.at[me], bs, br, peer).start()

    def send_ring(send, offsets):
        for o in offsets:
            for k in (0, 1):
                send(2 * at(o) + k, o)
                if 2 * o != chips:
                    send(2 * at(-o) + k, o)

    pl.semaphore_wait(barrier, n - 1 + ncol - 1)
    for o in (1, 3, 2):
        x_copy(o).start()

    send_cols(0, 1, partner, 0)
    send_ring(functools.partial(send_cols, 0, 1), range(chips // 2, 0, -1))
    users = usr[...].astype(F32) + 1.0
    seg_first = jnp.sum(jnp.where(is_first, users, 0.0), axis=1, keepdims=True)
    seg_last = jnp.sum(jnp.where(is_last, users, 0.0), axis=1, keepdims=True)
    lane = iota((rows, 128), 1)
    spread = jnp.where(lane == row_r, seg_first, 0.0) + jnp.where((lane == 8 + row_r) & (row_r < 4), seg_last, 0.0)
    own_rows = (iota((n, rows), 1) // 8 == iota((n, rows), 0)).astype(F32).astype(BF16)
    segs = dot(own_rows, spread.astype(BF16))
    for d in range(n):
        sgp[d] = segs[d : d + 1]

    send_seg(partner, 0)
    send_ring(send_seg, range(chips // 2, 0, -1))
    own_seg = pltpu.make_async_copy(sgp.at[me], sgr.at[me], lsem.at[1])
    own_seg.start()

    def x_whole(j0, j1, recv):
        part = tok.at[pl.ds(j0, j1 - j0)]
        return pltpu.make_async_remote_copy(
            src_ref=part, dst_ref=part, send_sem=xs, recv_sem=recv,
            device_id={"col": lax.rem(col + 1, ncol)}, device_id_type=MESH,
        )

    x_whole(1, 3, xr.at[0]).wait_recv()
    pack(1)
    pack(2)
    send_ring(functools.partial(send_cols, 1, 3), [8, 7])
    x_whole(3, 4, xr.at[1]).wait_recv()
    pack(3)
    send_ring(functools.partial(send_cols, 3, 4), [8, 7])
    send_cols(1, 4, partner, 0)
    send_ring(functools.partial(send_cols, 1, 4), range(chips // 2 - 2, 0, -1))
    own_pay = pltpu.make_async_copy(pay.at[me], rcv.at[me], lsem.at[2])
    own_pay.start()

    pltpu.make_async_copy(win_h, win, wsem.at[0]).wait()
    hidden = dot(tok[0], win[0:slab])
    for j in range(1, ncol):
        hidden += dot(tok[j], win[j * slab : (j + 1) * slab])
    out[...] = hidden.astype(BF16)

    low = iota((1, 8, 1), 1) < 4
    low8 = iota((8, 1), 0) < 4
    i24 = iota((ROWS, 128), 0)
    lane24 = iota((ROWS, 128), 1)
    want = jnp.where(i24 < 16, i24 & 7, 8 + (i24 & 3))
    is_a = (i24 < 8) | ((i24 >= 16) & (i24 < 20))
    own_seg.wait()
    whole(sgr, n - 1, gs, gr).wait_recv()
    for a in range(chips):
        zz = at(OFFSETS[a])
        seg = jnp.where(is_a, sgr[2 * zz], sgr[2 * zz + 1])
        seg = jnp.sum(jnp.where(lane24 == want, seg, 0.0), axis=1, keepdims=True)
        umat[a * ROWS : (a + 1) * ROWS, :] = jnp.where((lane24.astype(F32) == seg) & (lane24 > 0), 1.0, 0.0)
    slots = n * CAP
    users_all = umat[...].astype(BF16)
    pos_j = position(iota((1, slots), 1), z, chips)
    for a in range(0, chips, 4):
        part = slice(a * ROWS, (a + 4) * ROWS)
        pos_i = position(iota((4 * ROWS, 1), 0) + a * ROWS, z, chips)
        same = dot_nt(umat[part, :].astype(BF16), users_all) > 0.5
        okm[part, :] = jnp.where(same & (pos_j <= pos_i), 1.0, 0.0)

    weights[ncol].wait()
    own_pay.wait()
    def give_back(b0, b1):
        for a0 in range(b0, b1, 2):
            part = slice(a0 * ROWS, (a0 + 2) * ROWS)
            gated = layer_norm(mixed[part, :]) * joined[part, 0:WIDTH].astype(F32)
            for a in (a0 + 1, a0):
                zz = at(OFFSETS[a])
                g = gated[(a - a0) * ROWS : (a - a0 + 1) * ROWS]
                e_lo, e_hi = g[16:24, : WIDTH // 2], g[16:24, WIDTH // 2 :]
                rpay[2 * zz, :, 0:WIDTH] = g[0:8].astype(BF16)
                rpay[2 * zz, :, WIDTH:] = jnp.where(low8, e_lo, pltpu.roll(e_hi, 4, 0)).astype(BF16)
                rpay[2 * zz + 1, :, 0:WIDTH] = g[8:16].astype(BF16)
                rpay[2 * zz + 1, :, WIDTH:] = jnp.where(low8, pltpu.roll(e_lo, 4, 0), e_hi).astype(BF16)
                if a == 0:
                    send_back(partner, 0)
                else:
                    for k in (0, 1):
                        send_back(2 * zz + k, OFFSETS[a])

    for g, (a0, a1) in enumerate(GROUPS):
        whole(rcv, 2 * (a1 - a0) - (a0 == 0), fs, fr.at[g]).wait_recv()
        parts = []
        for a in range(a0, a1):
            zz = at(OFFSETS[a])
            va, vb = rcv[2 * zz].astype(F32), rcv[2 * zz + 1].astype(F32)
            ea, eb = va[:, :, slab:], vb[:, :, slab:]
            ex_lo = jnp.where(low, ea, pltpu.roll(eb, 4, 1))
            ex_hi = jnp.where(low, pltpu.roll(ea, 4, 1), eb)
            parts.append(jnp.concatenate([v[:, :, :slab] for v in (va, vb)] + [jnp.concatenate([ex_lo, ex_hi], axis=2)], axis=1))
        r0, r1 = a0 * ROWS, a1 * ROWS
        looked = jnp.concatenate(parts, axis=1).astype(BF16)
        projected = dot(looked[0], win[0:slab])
        for j in range(1, ncol):
            projected += dot(looked[j], win[j * slab : (j + 1) * slab])
        normed = layer_norm(projected.astype(BF16).astype(F32)).astype(BF16)

        def project(c0, c1, normed=normed, r0=r0, r1=r1):
            joined[r0:r1, c0:c1] = silu(dot(normed, wj[:, c0:c1])).astype(BF16)

        def add_new(q0, q1, h):
            hs = slice(h * HEAD_DIM, (h + 1) * HEAD_DIM)
            vs, qs, ks = (slice(c * WIDTH + hs.start, c * WIDTH + hs.stop) for c in (1, 2, 3))
            w = silu(dot_nt(joined[q0:q1, qs], joined[r0:r1, ks]), HEAD_DIM ** (-0.5))
            add = dot((w * okm[q0:q1, r0:r1]).astype(BF16), joined[r0:r1, vs])
            old = min(q1, r0)
            if old > q0:
                mixed[q0:old, hs] += add[: old - q0]
            if q1 > r0:
                if r0:
                    w = silu(dot_nt(joined[r0:r1, qs], joined[0:r0, ks]), HEAD_DIM ** (-0.5))
                    mixed[r0:r1, hs] = add[r0 - q0 :] + dot((w * okm[r0:r1, 0:r0]).astype(BF16), joined[0:r0, vs])
                else:
                    mixed[0:r1, hs] = add

        project(3 * WIDTH, 4 * WIDTH)
        project(WIDTH, 2 * WIDTH)
        q0 = 0
        if a1 == chips:
            q0 = GROUPS[0][1] * ROWS
            for h in range(HEADS):
                add_new(0, q0, h)
            give_back(0, GROUPS[0][1])
        project(2 * WIDTH, 3 * WIDTH)
        for h in range(HEADS):
            add_new(q0, r1, h)
            if h % 2 == 0:
                project(h * HEAD_DIM, (h + 2) * HEAD_DIM)

    give_back(GROUPS[0][1], chips)
    own_ret = pltpu.make_async_copy(rpay.at[me], rrcv.at[me], lsem.at[3])
    own_ret.start()

    tok_t = iota((tokens, n), 0).astype(F32)
    dest = (tok_t >= starts) & (tok_t < ends)
    owner = jnp.sum(jnp.where(dest, iota((tokens, n), 1).astype(F32), 0.0), axis=1, keepdims=True)
    slot = jnp.sum(jnp.where(dest, tok_t - starts, 0.0), axis=1, keepdims=True)
    lane_p = iota((tokens, rows), 1)
    lane_i = lane_p & 7
    here = (lane_p // 8).astype(F32) == owner
    lane_f = lane_i.astype(F32)
    take_first = (here & (lane_f == slot)).astype(F32).astype(BF16)
    take_lo = (here & (lane_i < 4) & (lane_f + 8.0 == slot)).astype(F32).astype(BF16)
    take_hi = (here & (lane_i >= 4) & (lane_f + 4.0 == slot)).astype(F32).astype(BF16)

    x_whole(1, ncol, xr.at[0]).wait_send()
    whole(sgp, n - 1, gs, gr).wait_send()
    whole(pay, n - 1, fs, fr.at[0]).wait_send()
    own_ret.wait()
    weights[ncol + 1].wait()

    whole(rrcv, n - 1, bs, br).wait_recv()
    back = rrcv[:, :, 0:WIDTH].astype(F32).reshape(rows, WIDTH).astype(BF16)
    back_x = rrcv[:, :, WIDTH:].astype(F32).reshape(rows, WIDTH // 2).astype(BF16)
    gated = dot(take_first, back)
    gated_lo = gated[:, : WIDTH // 2] + dot(take_lo, back_x)
    gated_hi = gated[:, WIDTH // 2 :] + dot(take_hi, back_x)
    branch = dot(gated_lo.astype(BF16), wo[: WIDTH // 2]) + dot(gated_hi.astype(BF16), wo[WIDTH // 2 :])
    out[...] = (out[...].astype(F32) + branch.astype(BF16).astype(F32)).astype(BF16)

    whole(rpay, n - 1, bs, br).wait_send()


def on_device(n, ncol, lookups, input_weight, joined_weight, output_weight, owner_counts, user_index):
    tokens = user_index.shape[0]
    dma = pltpu.SemaphoreType.DMA
    anyspace = pl.BlockSpec(memory_space=pl.ANY)
    vmem = pl.BlockSpec(memory_space=pltpu.VMEM)
    return pl.pallas_call(
        functools.partial(kernel, n, ncol),
        name="hstu",
        out_shape=pltpu.VMEM((tokens, D), BF16),
        in_specs=[anyspace] * 6,
        out_specs=vmem,
        scratch_shapes=[
            pltpu.VMEM((1, n), jnp.int32),
            pltpu.VMEM((1, tokens), jnp.int32),
            pltpu.VMEM((ncol, tokens, D // ncol), BF16),
            pltpu.VMEM((D, D), BF16),
            pltpu.VMEM((D, 4 * WIDTH), BF16),
            pltpu.VMEM((WIDTH, D), BF16),
            pltpu.VMEM((n, ncol, 8, 3 * D // 2 // ncol), BF16),
            pltpu.VMEM((n, ncol, 8, 3 * D // 2 // ncol), BF16),
            pltpu.VMEM((n, 1, 128), F32),
            pltpu.VMEM((n, 1, 128), F32),
            pltpu.VMEM((n * CAP, 4 * WIDTH), BF16),
            pltpu.VMEM((n * CAP, 128), F32),
            pltpu.VMEM((n * CAP, n * CAP), F32),
            pltpu.VMEM((n * CAP, WIDTH), F32),
            pltpu.VMEM((n, 8, 3 * WIDTH // 2), BF16),
            pltpu.VMEM((n, 8, 3 * WIDTH // 2), BF16),
            dma((3,)), dma((6,)), dma, dma((2,)), dma, dma, dma, dma((len(GROUPS),)), dma, dma,
        ],
        compiler_params=pltpu.CompilerParams(collective_id=0, has_side_effects=True),
    )(lookups, input_weight, joined_weight, output_weight, owner_counts, user_index.reshape(1, tokens))


def solution(mesh):
    return jax.shard_map(
        functools.partial(on_device, mesh.shape["batch"], mesh.shape["col"]),
        mesh=mesh,
        in_specs=(
            P(("rep", "batch"), "col"),
            P(),
            P(),
            P(),
            P(("rep", "batch", "col"), None),
            P(("rep", "batch", "col")),
        ),
        out_specs=P(("rep", "batch", "col"), None),
        check_vma=False,
    )
```

```python
import functools

import jax
import jax.numpy as jnp
from jax import lax
from jax.experimental import pallas as pl
from jax.experimental.pallas import tpu as pltpu
from jax.sharding import PartitionSpec as P

MESH = pl.DeviceIdType.MESH
HEADS = 4
HEAD_DIM = 128
WIDTH = HEADS * HEAD_DIM
D = 1024
CAP = 12
ROWS = 24
eps_norm = 1e-06
F32 = jnp.float32
BF16 = jnp.bfloat16

OFFSETS = [0, 8] + [s * o for o in range(7, 0, -1) for s in (1, -1)]
REL = (0, 1, 3, 2)
GROUPS = [(0, 6), (6, 10), (10, 16)]


def group_of(o):
    a = OFFSETS.index(abs(o))
    return [a0 <= a < a1 for a0, a1 in GROUPS].index(True)


def layer_norm(values):
    row_mean = jnp.mean(values, axis=-1, keepdims=True)
    centered = values - row_mean
    row_var = jnp.mean(centered * centered, axis=-1, keepdims=True)
    return centered * lax.rsqrt(row_var + eps_norm)


def silu(values, scale=1.0):
    half = values * (0.5 * scale)
    return half + half * jnp.tanh(half)


def dot(a, b):
    return jnp.dot(a, b, preferred_element_type=F32)


def dot_nt(a, b):
    return lax.dot_general(a, b, (((1,), (1,)), ((), ())), preferred_element_type=F32)


def iota(shape, dim):
    return lax.broadcasted_iota(jnp.int32, shape, dim)


def position(row, z, chips):
    a = row // ROWS
    i = row - a * ROWS
    step = jnp.where(a == 0, 0, chips // 2 - a // 2)
    off = jnp.where((a & 1) == 1, chips - step, step)
    zz = z + off
    zz = jnp.where(zz >= chips, zz - chips, zz)
    zz = jnp.where(zz >= chips, zz - chips, zz)
    second = jnp.where(i < 16, i // 8, (i - 16) // 4)
    slot = jnp.where(i < 16, i & 7, 8 + (i & 3))
    return (2 * zz + second) * CAP + slot


def kernel(
    n, ncol, lk, win_h, wj_h, wo_h, cnt_h, usr_h, out,
    cnt, usr, tok, win, wj, wo, pay, rcv, sgp, sgr, joined, umat, okm, mixed, rpay, rrcv,
    wsem, lsem, xs, xr, gs, gr, fs, fr, bs, br,
):
    me = lax.axis_index("batch")
    col = lax.axis_index("col")
    chips = n // 2
    z, core = me // 2, lax.rem(me, 2)
    tokens = usr.shape[1]
    barrier = pltpu.get_barrier_semaphore()
    partner = 2 * z + 1 - core
    slab = D // ncol

    def at(o):
        return lax.rem(z + o + chips, chips)

    def signal(sem, peer):
        pl.semaphore_signal(sem, inc=1, device_id={"batch": peer}, device_id_type=MESH)

    small = [pltpu.make_async_copy(cnt_h, cnt, lsem.at[4]), pltpu.make_async_copy(usr_h, usr, lsem.at[5])]
    for c in small:
        c.start()
    own_tok = pltpu.make_async_copy(lk.at[pl.ds(col * tokens, tokens)], tok.at[0], lsem.at[0])
    own_tok.start()
    def greet(i, carry):
        o = chips // 2 - i
        for k in (0, 1):
            signal(barrier, 2 * at(o) + k)
            signal(barrier, 2 * at(-o) + k)
        return carry

    for k in (0, 1):
        signal(barrier, 2 * at(chips // 2) + k)
    lax.fori_loop(1, chips // 2, greet, 0)
    for o in range(1, ncol):
        pl.semaphore_signal(barrier, inc=1, device_id={"col": lax.rem(col + o, ncol)}, device_id_type=MESH)
    signal(barrier, partner)

    weights = [
        pltpu.make_async_copy(
            win_h.at[pl.ds(lax.rem(col + REL[j], ncol) * slab, slab)], win.at[pl.ds(j * slab, slab)], wsem.at[0]
        )
        for j in range(ncol)
    ]
    weights.append(pltpu.make_async_copy(wj_h, wj, wsem.at[1]))
    weights.append(pltpu.make_async_copy(wo_h, wo, wsem.at[2]))
    for w in weights:
        w.start()

    def x_copy(o):
        peer = lax.rem(col + o, ncol)
        j = REL.index(ncol - o)
        return pltpu.make_async_remote_copy(
            src_ref=lk.at[pl.ds(peer * tokens, tokens)], dst_ref=tok.at[j], send_sem=xs, recv_sem=xr.at[j // 3],
            device_id={"col": peer}, device_id_type=MESH,
        )

    for c in small:
        c.wait()
    counts = cnt[...].astype(F32)
    upto = (iota((n, n), 0) <= iota((n, n), 1)).astype(F32).astype(BF16)
    ends = dot(jnp.broadcast_to(counts, (8, n)).astype(BF16), upto)[0:1]
    starts = ends - counts
    rows = 8 * n
    row_d, row_r = iota((rows, n), 0) // 8, iota((rows, 1), 0) & 7
    mine = row_d == iota((rows, n), 1)
    start_col = jnp.sum(jnp.where(mine, starts, 0.0), axis=1, keepdims=True)
    count_col = jnp.sum(jnp.where(mine, counts, 0.0), axis=1, keepdims=True)

    lane_t = iota((rows, tokens), 1).astype(F32)
    first_r = row_r.astype(F32)
    last_r = 8.0 + (row_r & 3).astype(F32)
    want_first = jnp.where(first_r < count_col, start_col + first_r, -1.0)
    want_last = jnp.where(last_r < count_col, start_col + last_r, -1.0)
    is_first = lane_t == want_first
    is_last = lane_t == want_last
    pick_first = is_first.astype(F32).astype(BF16)
    pick_last = is_last.astype(F32).astype(BF16)

    def pack(j):
        first = dot(pick_first, tok[j])
        last = dot(pick_last, tok[j])
        fold = jnp.where(row_r < 4, last[:, : slab // 2], last[:, slab // 2 :])
        pay[:, j, :, 0:slab] = first.reshape(n, 8, slab).astype(BF16)
        pay[:, j, :, slab:] = fold.reshape(n, 8, slab // 2).astype(BF16)

    own_tok.wait()
    pack(0)

    def copy(src, dst, send, recv, peer):
        return pltpu.make_async_remote_copy(
            src_ref=src, dst_ref=dst, send_sem=send, recv_sem=recv, device_id={"batch": peer}, device_id_type=MESH
        )

    def whole(buf, blocks, send, recv):
        return copy(buf.at[pl.ds(0, blocks)], buf.at[pl.ds(0, blocks)], send, recv, partner)

    def send_cols(j0, j1, peer, o):
        cols = pl.ds(j0, j1 - j0)
        copy(pay.at[peer, cols], rcv.at[me, cols], fs, fr.at[group_of(o)], peer).start()

    def send_seg(peer, o):
        copy(sgp.at[peer], sgr.at[me], gs, gr, peer).start()

    def send_back(peer, o):
        copy(rpay.at[peer], rrcv.at[me], bs, br, peer).start()

    def send_ring(send, offsets):
        for o in offsets:
            for k in (0, 1):
                send(2 * at(o) + k, o)
                if 2 * o != chips:
                    send(2 * at(-o) + k, o)

    pl.semaphore_wait(barrier, n - 1 + ncol - 1)
    for o in (1, 3, 2):
        x_copy(o).start()

    send_cols(0, 1, partner, 0)
    send_ring(functools.partial(send_cols, 0, 1), range(chips // 2, 0, -1))
    users = usr[...].astype(F32) + 1.0
    seg_first = jnp.sum(jnp.where(is_first, users, 0.0), axis=1, keepdims=True)
    seg_last = jnp.sum(jnp.where(is_last, users, 0.0), axis=1, keepdims=True)
    lane = iota((rows, 128), 1)
    spread = jnp.where(lane == row_r, seg_first, 0.0) + jnp.where((lane == 8 + row_r) & (row_r < 4), seg_last, 0.0)
    own_rows = (iota((n, rows), 1) // 8 == iota((n, rows), 0)).astype(F32).astype(BF16)
    segs = dot(own_rows, spread.astype(BF16))
    for d in range(n):
        sgp[d] = segs[d : d + 1]

    send_seg(partner, 0)
    send_ring(send_seg, range(chips // 2, 0, -1))
    own_seg = pltpu.make_async_copy(sgp.at[me], sgr.at[me], lsem.at[1])
    own_seg.start()

    def x_whole(j0, j1, recv):
        part = tok.at[pl.ds(j0, j1 - j0)]
        return pltpu.make_async_remote_copy(
            src_ref=part, dst_ref=part, send_sem=xs, recv_sem=recv,
            device_id={"col": lax.rem(col + 1, ncol)}, device_id_type=MESH,
        )

    x_whole(1, 3, xr.at[0]).wait_recv()
    pack(1)
    pack(2)
    send_ring(functools.partial(send_cols, 1, 3), [8, 7])
    x_whole(3, 4, xr.at[1]).wait_recv()
    pack(3)
    send_ring(functools.partial(send_cols, 3, 4), [8, 7])
    send_cols(1, 4, partner, 0)
    send_ring(functools.partial(send_cols, 1, 4), range(chips // 2 - 2, 0, -1))
    own_pay = pltpu.make_async_copy(pay.at[me], rcv.at[me], lsem.at[2])
    own_pay.start()

    pltpu.make_async_copy(win_h, win, wsem.at[0]).wait()
    hidden = dot(tok[0], win[0:slab])
    for j in range(1, ncol):
        hidden += dot(tok[j], win[j * slab : (j + 1) * slab])
    out[...] = hidden.astype(BF16)

    low = iota((1, 8, 1), 1) < 4
    low8 = iota((8, 1), 0) < 4
    i24 = iota((ROWS, 128), 0)
    lane24 = iota((ROWS, 128), 1)
    want = jnp.where(i24 < 16, i24 & 7, 8 + (i24 & 3))
    is_a = (i24 < 8) | ((i24 >= 16) & (i24 < 20))
    own_seg.wait()
    whole(sgr, n - 1, gs, gr).wait_recv()
    for a in range(chips):
        zz = at(OFFSETS[a])
        seg = jnp.where(is_a, sgr[2 * zz], sgr[2 * zz + 1])
        seg = jnp.sum(jnp.where(lane24 == want, seg, 0.0), axis=1, keepdims=True)
        umat[a * ROWS : (a + 1) * ROWS, :] = jnp.where((lane24.astype(F32) == seg) & (lane24 > 0), 1.0, 0.0)
    slots = n * CAP
    users_all = umat[...].astype(BF16)
    pos_j = position(iota((1, slots), 1), z, chips)
    for a in range(0, chips, 4):
        part = slice(a * ROWS, (a + 4) * ROWS)
        pos_i = position(iota((4 * ROWS, 1), 0) + a * ROWS, z, chips)
        same = dot_nt(umat[part, :].astype(BF16), users_all) > 0.5
        okm[part, :] = jnp.where(same & (pos_j <= pos_i), 1.0, 0.0)

    weights[ncol].wait()
    own_pay.wait()
    def give_back(b0, b1):
        for a0 in range(b0, b1, 2):
            part = slice(a0 * ROWS, (a0 + 2) * ROWS)
            gated = layer_norm(mixed[part, :]) * joined[part, 0:WIDTH].astype(F32)
            for a in (a0 + 1, a0):
                zz = at(OFFSETS[a])
                g = gated[(a - a0) * ROWS : (a - a0 + 1) * ROWS]
                e_lo, e_hi = g[16:24, : WIDTH // 2], g[16:24, WIDTH // 2 :]
                rpay[2 * zz, :, 0:WIDTH] = g[0:8].astype(BF16)
                rpay[2 * zz, :, WIDTH:] = jnp.where(low8, e_lo, pltpu.roll(e_hi, 4, 0)).astype(BF16)
                rpay[2 * zz + 1, :, 0:WIDTH] = g[8:16].astype(BF16)
                rpay[2 * zz + 1, :, WIDTH:] = jnp.where(low8, pltpu.roll(e_lo, 4, 0), e_hi).astype(BF16)
                if a == 0:
                    send_back(partner, 0)
                else:
                    for k in (0, 1):
                        send_back(2 * zz + k, OFFSETS[a])

    far = GROUPS[0][1] * ROWS

    def attend(q0, q1, k0, k1, h, add):
        hs = slice(h * HEAD_DIM, (h + 1) * HEAD_DIM)
        vs, qs, ks = (slice(c * WIDTH + hs.start, c * WIDTH + hs.stop) for c in (1, 2, 3))
        w = silu(dot_nt(joined[q0:q1, qs], joined[k0:k1, ks]), HEAD_DIM ** (-0.5))
        new = dot((w * okm[q0:q1, k0:k1]).astype(BF16), joined[k0:k1, vs])
        mixed[q0:q1, hs] = mixed[q0:q1, hs] + new if add else new

    for g, (a0, a1) in enumerate(GROUPS):
        whole(rcv, 2 * (a1 - a0) - (a0 == 0), fs, fr.at[g]).wait_recv()
        parts = []
        for a in range(a0, a1):
            zz = at(OFFSETS[a])
            va, vb = rcv[2 * zz].astype(F32), rcv[2 * zz + 1].astype(F32)
            ea, eb = va[:, :, slab:], vb[:, :, slab:]
            ex_lo = jnp.where(low, ea, pltpu.roll(eb, 4, 1))
            ex_hi = jnp.where(low, pltpu.roll(ea, 4, 1), eb)
            parts.append(jnp.concatenate([v[:, :, :slab] for v in (va, vb)] + [jnp.concatenate([ex_lo, ex_hi], axis=2)], axis=1))
        r0, r1 = a0 * ROWS, a1 * ROWS
        looked = jnp.concatenate(parts, axis=1).astype(BF16)
        projected = dot(looked[0], win[0:slab])
        for j in range(1, ncol):
            projected += dot(looked[j], win[j * slab : (j + 1) * slab])
        normed = layer_norm(projected.astype(BF16).astype(F32)).astype(BF16)

        def project(c0, c1, normed=normed, r0=r0, r1=r1):
            joined[r0:r1, c0:c1] = silu(dot(normed, wj[:, c0:c1])).astype(BF16)

        project(3 * WIDTH, 4 * WIDTH)
        project(WIDTH, 2 * WIDTH)
        if a0 == 0:
            project(2 * WIDTH, 3 * WIDTH)
        for h in range(HEADS):
            attend(0, far, r0, r1, h, g > 0)
            if a0 == 0 and h % 2 == 0:
                project(h * HEAD_DIM, (h + 2) * HEAD_DIM)
        if a1 == chips:
            give_back(0, GROUPS[0][1])
        if a0:
            project(2 * WIDTH, 3 * WIDTH)
            if a1 < chips:
                project(0, WIDTH)

    for h in range(HEADS):
        attend(far, n * CAP, 0, n * CAP, h, False)
        if h % 2 == 0:
            project(h * HEAD_DIM, (h + 2) * HEAD_DIM)
    give_back(GROUPS[0][1], chips)
    own_ret = pltpu.make_async_copy(rpay.at[me], rrcv.at[me], lsem.at[3])
    own_ret.start()

    tok_t = iota((tokens, n), 0).astype(F32)
    dest = (tok_t >= starts) & (tok_t < ends)
    owner = jnp.sum(jnp.where(dest, iota((tokens, n), 1).astype(F32), 0.0), axis=1, keepdims=True)
    slot = jnp.sum(jnp.where(dest, tok_t - starts, 0.0), axis=1, keepdims=True)
    lane_p = iota((tokens, rows), 1)
    lane_i = lane_p & 7
    here = (lane_p // 8).astype(F32) == owner
    lane_f = lane_i.astype(F32)
    take_first = (here & (lane_f == slot)).astype(F32).astype(BF16)
    take_lo = (here & (lane_i < 4) & (lane_f + 8.0 == slot)).astype(F32).astype(BF16)
    take_hi = (here & (lane_i >= 4) & (lane_f + 4.0 == slot)).astype(F32).astype(BF16)

    x_whole(1, ncol, xr.at[0]).wait_send()
    whole(sgp, n - 1, gs, gr).wait_send()
    whole(pay, n - 1, fs, fr.at[0]).wait_send()
    own_ret.wait()
    weights[ncol + 1].wait()

    whole(rrcv, n - 1, bs, br).wait_recv()
    back = rrcv[:, :, 0:WIDTH].astype(F32).reshape(rows, WIDTH).astype(BF16)
    back_x = rrcv[:, :, WIDTH:].astype(F32).reshape(rows, WIDTH // 2).astype(BF16)
    gated = dot(take_first, back)
    gated_lo = gated[:, : WIDTH // 2] + dot(take_lo, back_x)
    gated_hi = gated[:, WIDTH // 2 :] + dot(take_hi, back_x)
    branch = dot(gated_lo.astype(BF16), wo[: WIDTH // 2]) + dot(gated_hi.astype(BF16), wo[WIDTH // 2 :])
    out[...] = (out[...].astype(F32) + branch.astype(BF16).astype(F32)).astype(BF16)

    whole(rpay, n - 1, bs, br).wait_send()


def on_device(n, ncol, lookups, input_weight, joined_weight, output_weight, owner_counts, user_index):
    tokens = user_index.shape[0]
    dma = pltpu.SemaphoreType.DMA
    anyspace = pl.BlockSpec(memory_space=pl.ANY)
    vmem = pl.BlockSpec(memory_space=pltpu.VMEM)
    return pl.pallas_call(
        functools.partial(kernel, n, ncol),
        name="hstu",
        out_shape=pltpu.VMEM((tokens, D), BF16),
        in_specs=[anyspace] * 6,
        out_specs=vmem,
        scratch_shapes=[
            pltpu.VMEM((1, n), jnp.int32),
            pltpu.VMEM((1, tokens), jnp.int32),
            pltpu.VMEM((ncol, tokens, D // ncol), BF16),
            pltpu.VMEM((D, D), BF16),
            pltpu.VMEM((D, 4 * WIDTH), BF16),
            pltpu.VMEM((WIDTH, D), BF16),
            pltpu.VMEM((n, ncol, 8, 3 * D // 2 // ncol), BF16),
            pltpu.VMEM((n, ncol, 8, 3 * D // 2 // ncol), BF16),
            pltpu.VMEM((n, 1, 128), F32),
            pltpu.VMEM((n, 1, 128), F32),
            pltpu.VMEM((n * CAP, 4 * WIDTH), BF16),
            pltpu.VMEM((n * CAP, 128), F32),
            pltpu.VMEM((n * CAP, n * CAP), F32),
            pltpu.VMEM((n * CAP, WIDTH), F32),
            pltpu.VMEM((n, 8, 3 * WIDTH // 2), BF16),
            pltpu.VMEM((n, 8, 3 * WIDTH // 2), BF16),
            dma((3,)), dma((6,)), dma, dma((2,)), dma, dma, dma, dma((len(GROUPS),)), dma, dma,
        ],
        compiler_params=pltpu.CompilerParams(collective_id=0, has_side_effects=True),
    )(lookups, input_weight, joined_weight, output_weight, owner_counts, user_index.reshape(1, tokens))


def solution(mesh):
    return jax.shard_map(
        functools.partial(on_device, mesh.shape["batch"], mesh.shape["col"]),
        mesh=mesh,
        in_specs=(
            P(("rep", "batch"), "col"),
            P(),
            P(),
            P(),
            P(("rep", "batch", "col"), None),
            P(("rep", "batch", "col")),
        ),
        out_specs=P(("rep", "batch", "col"), None),
        check_vma=False,
    )
```
